128 devices in a mesh: samp: 32 (over z, y, core), var: 4 (over x).
Axes of the slice: x: 4, y: 4, z: 4, core: 2. Of those that a mesh axis runs over, the one named last changes fastest.
Arguments:
- geno: int32 [65536, 8192], P('samp', 'var'), may hold values from 0 to 2, as said below
- allele_pct: int32 [8192], P('var'), may hold values from 5 to 50
- test_geno: int32 [65536, 2048], P('samp', 'var'), may hold values from 0 to 2, as said below
- test_pct: int32 [2048], P('var'), may hold values from 5 to 50
- exposure: float32 [65536], P('samp'), may hold values from -4 to 4
- perm: int32 [8, 65536], P(None, 'samp'), may hold values from 0 to 65535, each once within a row
- var_comp: float32 [3], replicated, may hold values from 0.3 to 1.5
- solution: float32 [8, 65536], P(None, 'samp'), may hold values from -6 to 6
- resid: float32 [8, 65536], P(None, 'samp'), may hold values from -32 to 32
- direction: float32 [8, 65536], P(None, 'samp'), may hold values from -32 to 32
Outputs:
- new_solution: float32 [8, 65536], P(None, 'samp')
- new_resid: float32 [8, 65536], P(None, 'samp')
- new_direction: float32 [8, 65536], P(None, 'samp')
- assoc_scores: float32 [16, 2048], P(None, 'var')
The draws below stay inside these ranges and needn't reach their ends.
Inputs may be any that keep to these rules, and one draw needn't show every extreme that they name: `geno`: dosages of a variant follow its allele frequency. `test_geno`: dosages of a variant follow its allele frequency.
All inputs are finite; a program needn't handle non-finite values.
Results may differ from the reference program's by a relative error of at most 0.00016.
Values sent between devices are 32-bit elements; how exact they have to be, the bound alone decides.
A program may use at most 64 MiB of HBM per device.

```python
import math
import jax
import jax.numpy as jnp
from jax import lax

SLAB = 8192
TESTV = 2048
RHS = 8
NS = 65536


def dosage_table(key, code, width):
    pct = jax.random.randint(jax.random.fold_in(key, code), (width,), 5, 51)
    draws = jax.random.randint(jax.random.fold_in(key, code + 1), (NS, width), 0, 10000)
    upper = 10000 - (100 - pct) * (100 - pct)
    double = pct * pct
    codes = (draws < upper[None, :]).astype(jnp.int32) + (draws < double[None, :]).astype(jnp.int32)
    return (pct.astype(jnp.int32), codes)


def draw_geno(key, part):
    return dosage_table(key, 101, SLAB)[1]


def draw_allele_pct(key, part):
    return dosage_table(key, 101, SLAB)[0]


def draw_test_geno(key, part):
    return dosage_table(key, 303, TESTV)[1]


def draw_test_pct(key, part):
    return dosage_table(key, 303, TESTV)[0]


def scaled_rows(key):
    position = jnp.arange(NS, dtype=jnp.float32) / max(NS - 1, 1)
    spread = jnp.exp(jax.random.uniform(jax.random.fold_in(key, 1), (NS,), jnp.float32, 0.0, 1.0) * math.log(10.0))
    column = jax.random.uniform(jax.random.fold_in(key, 2), (RHS, 1), jnp.float32, 0.5, 2.0)
    base = 0.1 * (1.0 + 2.0 * position) * spread
    values = jnp.clip(jax.random.normal(jax.random.fold_in(key, 4), (RHS, NS), jnp.float32), -4.0, 4.0)
    values = values * base[None, :] * column
    return values.astype(jnp.float32)


def draw_resid(key, part):
    return scaled_rows(jax.random.fold_in(key, 11))


def draw_direction(key, part):
    return scaled_rows(jax.random.fold_in(key, 23))


def level_of(own_key, extent, pieces, low, top_value):
    def one(dim, shards_of):
        heights = jax.random.uniform(jax.random.fold_in(jax.random.fold_in(own_key, 6), dim), (shards_of,), jnp.float32, low / len(pieces), top_value / len(pieces))
        return jnp.repeat(jnp.exp(heights), extent[dim] // shards_of).reshape((-1,) + (1,) * (len(extent) - dim - 1))

    factor_of = one(*pieces[0])
    for cut in pieces[1:]:
        factor_of = factor_of * one(*cut)
    return factor_of


def normal_values(stream_key, shape, scale, limit, cuts=(), kind=jnp.bfloat16):
    entries = jax.random.normal(stream_key, shape, jnp.float32) * scale
    if len(cuts) > 0:
        entries = level_of(stream_key, shape, cuts, -0.22, 0.18) * entries
    return jnp.clip(entries, min=-limit, max=limit).astype(kind)


def setup_inputs(seed: int = 0) -> dict:
    arg_keys = jax.random.split(jax.random.key(seed), 11)
    geno = draw_geno(jax.random.fold_in(arg_keys[10], 71), 0)
    allele_pct = draw_allele_pct(jax.random.fold_in(arg_keys[10], 71), 0)
    test_geno = draw_test_geno(jax.random.fold_in(arg_keys[10], 71), 0)
    test_pct = draw_test_pct(jax.random.fold_in(arg_keys[10], 71), 0)
    exposure = normal_values(arg_keys[4], (NS,), 1.0, 4.0, ((0, 32),), jnp.float32)
    perm = jax.vmap(lambda own: jax.random.permutation(own, NS))(jax.random.split(arg_keys[5], RHS)).reshape((RHS, NS)).astype(jnp.int32)
    var_comp = jnp.clip(jax.random.uniform(arg_keys[6], (3,), jnp.float32, 0.3, 1.5), 0.3, 1.5)
    solution = normal_values(arg_keys[7], (RHS, NS), 1.0, 6.0, ((1, 32),), jnp.float32)
    resid = draw_resid(jax.random.fold_in(arg_keys[10], 71), 0)
    direction = draw_direction(jax.random.fold_in(arg_keys[10], 71), 0)
    return dict(geno=geno, allele_pct=allele_pct, test_geno=test_geno, test_pct=test_pct, exposure=exposure, perm=perm, var_comp=var_comp, solution=solution, resid=resid, direction=direction)


def standardize(codes, pct):
    freq = pct.astype(jnp.float32) / 100.0
    return (codes.astype(jnp.float32) - 2.0 * freq) * lax.rsqrt(2.0 * freq * (1.0 - freq))

def reference(geno, allele_pct, test_geno, test_pct, exposure, perm, var_comp, solution, resid, direction):
    highest = lax.Precision.HIGHEST
    shuffled = exposure[perm]
    stacked = jnp.concatenate([direction, shuffled * direction], axis=0)
    block = math.gcd(SLAB, 1024)

    def add_block(index, total):
        start = index * block
        codes = lax.dynamic_slice_in_dim(geno, start, block, 1)
        pct = lax.dynamic_slice_in_dim(allele_pct, start, block, 0)
        loadings = standardize(codes, pct)
        weights = jnp.dot(stacked, loadings, precision=highest, preferred_element_type=jnp.float32)
        return total + lax.dot_general(weights, loadings, (((1,), (1,)), ((), ())), precision=highest, preferred_element_type=jnp.float32)
    kernel_rows = lax.fori_loop(0, SLAB // block, add_block, jnp.zeros((2 * RHS, NS), jnp.float32))
    image = var_comp[0] * direction + (var_comp[1] * kernel_rows[:RHS] + var_comp[2] * shuffled * kernel_rows[RHS:]) / SLAB
    norm_now = lax.optimization_barrier(jnp.sum(resid * resid, axis=1))
    curvature = lax.optimization_barrier(jnp.sum(direction * image, axis=1))
    alpha = norm_now / curvature
    new_solution = solution + alpha[:, None] * direction
    new_resid = resid - alpha[:, None] * image
    norm_next = lax.optimization_barrier(jnp.sum(new_resid * new_resid, axis=1))
    new_direction = new_resid + (norm_next / norm_now)[:, None] * direction
    markers = standardize(test_geno, test_pct)
    stacked_resid = jnp.concatenate([new_resid, shuffled * new_resid], axis=0)
    assoc_scores = jnp.dot(stacked_resid, markers, precision=highest, preferred_element_type=jnp.float32) / math.sqrt(NS)
    return (new_solution, new_resid, new_direction, assoc_scores)
```

```python
import functools

import jax
import jax.numpy as jnp
from jax import lax
from jax.experimental import pallas as pl
from jax.experimental.pallas import tpu as pltpu
from jax.sharding import PartitionSpec as P

MESH = pl.DeviceIdType.MESH
F32 = jnp.float32
BF16 = jnp.bfloat16


def log2(n):
    return n.bit_length() - 1


def split3(value):
    high = value.astype(BF16)
    rest = value - high.astype(F32)
    mid = rest.astype(BF16)
    low = (rest - mid.astype(F32)).astype(BF16)
    return high, mid, low


def sum3(value):
    rows = value.shape[0] // 3
    return value[:rows] + value[rows : 2 * rows] + value[2 * rows :]


def kernel(
    dims,
    geno_hbm, tgeno_hbm, pct_ref, tpct_ref, expo_ref, perm_ref, vc_ref, sol_ref, res_ref, dir_ref,
    osol_ref, ores_ref, odir_ref, oassoc_ref,
    graw, traw, gbf, tbf, table, tparts, shuf, parts, apart,
    psend, precv, pz, pall, qsend, qrecv, imgs, fsend, frecv, fz, fall,
    gsem, tsem, sem_ez, sem_ej, sem_sh, sem_p, sem_pz, sem_pa, sem_q, sem_im, sem_f, sem_fz, sem_fa,
):
    NZ, NJ, NX, scale_rows = dims
    samp = lax.axis_index("samp")
    x = lax.axis_index("var")
    z = samp // NJ
    j = samp % NJ
    SP = dir_ref.shape[1]
    V = pct_ref.shape[1]
    TV = tpct_ref.shape[1]
    RP = SP // 128
    VB = V // NJ
    SQ = SP // NX
    chunks = graw.shape[0]
    crows = graw.shape[1]
    tchunks = traw.shape[0]
    trows = traw.shape[1]

    for i in range(chunks):
        pltpu.make_async_copy(geno_hbm.at[pl.ds(i * crows, crows), :], graw.at[i], gsem.at[i]).start()
    for i in range(tchunks):
        pltpu.make_async_copy(tgeno_hbm.at[pl.ds(i * trows, trows), :], traw.at[i], tsem.at[i]).start()

    def to_j(peer):
        return {"samp": z * NJ + peer}

    def to_z(peer):
        return {"samp": peer * NJ + j}

    def to_x(peer):
        return {"var": peer}

    groups = {"j": (j, NJ, to_j), "z": (z, NZ, to_z), "x": (x, NX, to_x)}

    def each_peer(group, body):
        me, count, _ = groups[group]

        def step(off, carry):
            body((me + off) % count)
            return carry

        lax.fori_loop(1, count, step, 0)

    def push(group, src, dst, sem, peer):
        me, _, place = groups[group]
        pltpu.make_async_remote_copy(
            src_ref=src, dst_ref=dst, send_sem=sem.at[0, peer], recv_sem=sem.at[1, me],
            device_id=place(peer), device_id_type=MESH,
        ).start()

    def arrived(group, dst_of, sem):
        me, _, place = groups[group]

        def one(peer):
            pltpu.make_async_remote_copy(
                src_ref=dst_of(peer), dst_ref=dst_of(peer), send_sem=sem.at[0, peer], recv_sem=sem.at[1, peer],
                device_id=place(peer), device_id_type=MESH,
            ).wait_recv()

        each_peer(group, one)

    def sent(group, src_of, sem):
        _, _, place = groups[group]

        def one(peer):
            pltpu.make_async_remote_copy(
                src_ref=src_of(peer), dst_ref=src_of(peer), send_sem=sem.at[0, peer], recv_sem=sem.at[1, peer],
                device_id=place(peer), device_id_type=MESH,
            ).wait_send()

        each_peer(group, one)

    barrier = pltpu.get_barrier_semaphore()
    for group in ("j", "z", "x"):
        place = groups[group][2]
        each_peer(group, lambda peer, place=place: pl.semaphore_signal(barrier, inc=1, device_id=place(peer), device_id_type=MESH))
    pl.semaphore_wait(barrier, NJ + NZ + NX - 3)

    each_peer("z", lambda peer: push("z", expo_ref, table.at[j, z], sem_ez, peer))
    table[j, z] = expo_ref[...]

    pct = pct_ref[...].astype(F32)
    tpct = tpct_ref[...].astype(F32)

    def convert(i):
        pltpu.make_async_copy(geno_hbm.at[pl.ds(i * crows, crows), :], graw.at[i], gsem.at[i]).wait()
        block = 32

        def rows(r, carry):
            start = pl.multiple_of(r * block, block)
            codes = graw[i, pl.ds(start, block), :].astype(F32)
            gbf[pl.ds(pl.multiple_of(i * crows + start, block), block), :] = (codes * 50.0 - pct).astype(BF16)
            return carry

        lax.fori_loop(0, crows // block, rows, 0)

    def tconvert(i):
        pltpu.make_async_copy(tgeno_hbm.at[pl.ds(i * trows, trows), :], traw.at[i], tsem.at[i]).wait()
        block = 64

        def rows(r, carry):
            start = pl.multiple_of(r * block, block)
            codes = traw[i, pl.ds(start, block), :].astype(F32)
            tbf[pl.ds(pl.multiple_of(i * trows + start, block), block), :] = (codes * 50.0 - tpct).astype(BF16)
            return carry

        lax.fori_loop(0, trows // block, rows, 0)

    half = chunks // 2

    def convert_step(i, carry):
        convert(i)
        return carry

    def tconvert_step(i, carry):
        tconvert(i)
        return carry

    lax.fori_loop(0, half, convert_step, 0)

    arrived("z", lambda peer: table.at[j, peer], sem_ez)
    each_peer("j", lambda peer: push("j", table.at[j], table.at[j], sem_ej, peer))

    lax.fori_loop(half, chunks, convert_step, 0)
    lax.fori_loop(0, tchunks, tconvert_step, 0)

    arrived("j", lambda peer: table.at[peer], sem_ej)

    rows_all = NJ * NZ * RP
    flat = table[...].reshape(rows_all, 128)
    high, mid, low = split3(flat.T)
    tparts[0:128, :] = high
    tparts[128:256, :] = mid
    tparts[256:384, :] = low
    index = perm_ref[:, pl.ds(pl.multiple_of(x * SQ, SQ), SQ)]
    row_z = index >> log2(SP * NJ)
    row_j = (index >> log2(SP)) & (NJ - 1)
    row_r = (index >> 7) & (RP - 1)
    row_of = (row_j * NZ + row_z) * RP + row_r
    lane_of = index & 127
    width = min(SQ, 256)
    for b in range(8):
        for c in range(SQ // width):
            cols = slice(c * width, (c + 1) * width)
            hit = lax.broadcasted_iota(jnp.int32, (rows_all, width), 0) == row_of[b : b + 1, cols]
            onehot = jnp.where(hit, 1.0, 0.0).astype(BF16)
            picked = sum3(jnp.dot(tparts[...], onehot, preferred_element_type=F32))
            lane_hit = lax.broadcasted_iota(jnp.int32, (128, width), 0) == lane_of[b : b + 1, cols]
            shuf[x, b : b + 1, cols] = jnp.sum(jnp.where(lane_hit, picked, 0.0), axis=0, keepdims=True)
    each_peer("x", lambda peer: push("x", shuf.at[x], shuf.at[x], sem_sh, peer))
    arrived("x", lambda peer: shuf.at[peer], sem_sh)

    def fill(value_of):
        for q in range(NX):
            value = value_of(q)
            stacked = jnp.concatenate([value, shuf[q] * value], axis=0)
            high, mid, low = split3(stacked)
            cols = slice(q * SQ, (q + 1) * SQ)
            parts[0:16, cols] = high
            parts[16:32, cols] = mid
            parts[32:48, cols] = low

    fill(lambda q: dir_ref[:, q * SQ : (q + 1) * SQ])

    def product(block):
        cols = pl.ds(pl.multiple_of(block * VB, VB), VB)
        return sum3(jnp.dot(parts[...], gbf[:, cols], preferred_element_type=F32))

    def product_step(peer):
        psend[peer] = product(peer)
        push("j", psend.at[peer], precv.at[j], sem_p, peer)

    each_peer("j", product_step)
    precv[j] = product(j)

    fill(lambda q: res_ref[:, q * SQ : (q + 1) * SQ])
    apart[...] = sum3(jnp.dot(parts[...], tbf[...], preferred_element_type=F32))

    arrived("j", lambda peer: precv.at[peer], sem_p)
    total = precv[0]
    for i in range(1, NJ):
        total = total + precv[i]
    pz[z] = total
    each_peer("z", lambda peer: push("z", pz.at[z], pz.at[z], sem_pz, peer))
    arrived("z", lambda peer: pz.at[peer], sem_pz)
    total = pz[0]
    for i in range(1, NZ):
        total = total + pz[i]
    pall[j] = total
    each_peer("j", lambda peer: push("j", pall.at[j], pall.at[j], sem_pa, peer))
    freq = pct / 100.0
    square = 1.0 / (2.0 * freq * (1.0 - freq)) / 2500.0
    arrived("j", lambda peer: pall.at[peer], sem_pa)

    for i in range(NJ):
        cols = slice(i * VB, (i + 1) * VB)
        high, mid, low = split3(pall[i] * square[:, cols])
        parts[0:16, cols] = high
        parts[16:32, cols] = mid
        parts[32:48, cols] = low

    def back(part):
        rows = pl.ds(pl.multiple_of(part * SQ, SQ), SQ)
        return sum3(
            lax.dot_general(parts[...], gbf[rows, :], (((1,), (1,)), ((), ())), preferred_element_type=F32)
        )

    def back_step(peer):
        qsend[peer] = back(peer)
        push("x", qsend.at[peer], qrecv.at[x], sem_q, peer)

    each_peer("x", back_step)
    qrecv[x] = back(x)
    arrived("x", lambda peer: qrecv.at[peer], sem_q)
    rows_sum = qrecv[0]
    for i in range(1, NX):
        rows_sum = rows_sum + qrecv[i]
    own_dir = dir_ref[:, pl.ds(pl.multiple_of(x * SQ, SQ), SQ)]
    imgs[x] = vc_ref[0] * own_dir + (vc_ref[1] * rows_sum[0:8] + vc_ref[2] * shuf[x] * rows_sum[8:16]) * (1.0 / scale_rows)
    each_peer("x", lambda peer: push("x", imgs.at[x], imgs.at[x], sem_im, peer))
    arrived("x", lambda peer: imgs.at[peer], sem_im)

    fill(lambda q: imgs[q])
    bpart = sum3(jnp.dot(parts[...], tbf[...], preferred_element_type=F32))
    sums = [jnp.zeros((8, 1), F32) for _ in range(4)]
    for q in range(NX):
        cols = slice(q * SQ, (q + 1) * SQ)
        d, r, im = dir_ref[:, cols], res_ref[:, cols], imgs[q]
        for k, term in enumerate((r * r, d * im, r * im, im * im)):
            sums[k] = sums[k] + jnp.sum(term, axis=1, keepdims=True)
    lane = lax.broadcasted_iota(jnp.int32, (8, 128), 1)
    scalars = jnp.where(lane == 0, sums[0], jnp.where(lane == 1, sums[1], jnp.where(lane == 2, sums[2], sums[3])))
    quarters = TV // 128
    for i in range(NJ):
        h, q = divmod(i, quarters)
        fsend[i, 0] = apart[8 * h : 8 * h + 8, 128 * q : 128 * q + 128]
        fsend[i, 1] = bpart[8 * h : 8 * h + 8, 128 * q : 128 * q + 128]
        fsend[i, 2] = scalars
    each_peer("j", lambda peer: push("j", fsend.at[peer], frecv.at[j], sem_f, peer))
    frecv[j] = fsend[j]
    arrived("j", lambda peer: frecv.at[peer], sem_f)
    total = frecv[0]
    for i in range(1, NJ):
        total = total + frecv[i]
    fz[z] = total
    each_peer("z", lambda peer: push("z", fz.at[z], fz.at[z], sem_fz, peer))
    arrived("z", lambda peer: fz.at[peer], sem_fz)
    total = fz[0]
    for i in range(1, NZ):
        total = total + fz[i]
    norm_now = total[2][:, 0:1]
    curvature = total[2][:, 1:2]
    alpha = norm_now / curvature
    fall[j] = total[0] - alpha * total[1]
    each_peer("j", lambda peer: push("j", fall.at[j], fall.at[j], sem_fa, peer))

    norm_next = norm_now - 2.0 * alpha * total[2][:, 2:3] + alpha * alpha * total[2][:, 3:4]
    beta = norm_next / norm_now
    for q in range(NX):
        cols = slice(q * SQ, (q + 1) * SQ)
        d = dir_ref[:, cols]
        new_res = res_ref[:, cols] - alpha * imgs[q]
        osol_ref[:, cols] = sol_ref[:, cols] + alpha * d
        ores_ref[:, cols] = new_res
        odir_ref[:, cols] = new_res + beta * d

    tfreq = tpct / 100.0
    root = (scale_rows_root(dims, SP)) * 50.0
    tscale = lax.rsqrt(2.0 * tfreq * (1.0 - tfreq)) / root
    arrived("j", lambda peer: fall.at[peer], sem_fa)
    for i in range(NJ):
        h, q = divmod(i, quarters)
        cols = slice(128 * q, 128 * q + 128)
        oassoc_ref[8 * h : 8 * h + 8, cols] = fall[i] * tscale[:, cols]

    sent("z", lambda peer: expo_ref, sem_ez)
    sent("j", lambda peer: table.at[j], sem_ej)
    sent("x", lambda peer: shuf.at[x], sem_sh)
    sent("j", lambda peer: psend.at[peer], sem_p)
    sent("z", lambda peer: pz.at[z], sem_pz)
    sent("j", lambda peer: pall.at[j], sem_pa)
    sent("x", lambda peer: qsend.at[peer], sem_q)
    sent("x", lambda peer: imgs.at[x], sem_im)
    sent("j", lambda peer: fsend.at[peer], sem_f)
    sent("z", lambda peer: fz.at[z], sem_fz)
    sent("j", lambda peer: fall.at[j], sem_fa)


def scale_rows_root(dims, per_device):
    return float(dims[0] * dims[1] * per_device) ** 0.5


def local(dims, geno, allele_pct, test_geno, test_pct, exposure, perm, var_comp, solution, resid, direction):
    NZ, NJ, NX, _ = dims
    SP, V = geno.shape
    TV = test_geno.shape[1]
    RP, VB, SQ = SP // 128, V // NJ, SP // NX
    chunks, tchunks = 8, 2
    vmem = pl.BlockSpec(memory_space=pltpu.VMEM)
    hbm = pl.BlockSpec(memory_space=pl.ANY)
    smem = pl.BlockSpec(memory_space=pltpu.SMEM)
    dma = pltpu.SemaphoreType.DMA
    rhs = jax.ShapeDtypeStruct((8, SP), F32)
    return pl.pallas_call(
        functools.partial(kernel, dims),
        out_shape=(rhs, rhs, rhs, jax.ShapeDtypeStruct((16, TV), F32)),
        in_specs=[hbm, hbm, vmem, vmem, vmem, vmem, smem, vmem, vmem, vmem],
        out_specs=(vmem, vmem, vmem, vmem),
        scratch_shapes=[
            pltpu.VMEM((chunks, SP // chunks, V), jnp.int32),
            pltpu.VMEM((tchunks, SP // tchunks, TV), jnp.int32),
            pltpu.VMEM((SP, V), BF16),
            pltpu.VMEM((SP, TV), BF16),
            pltpu.VMEM((NJ, NZ, RP, 128), F32),
            pltpu.VMEM((384, NJ * NZ * RP), BF16),
            pltpu.VMEM((NX, 8, SQ), F32),
            pltpu.VMEM((48, max(SP, V)), BF16),
            pltpu.VMEM((16, TV), F32),
            pltpu.VMEM((NJ, 16, VB), F32),
            pltpu.VMEM((NJ, 16, VB), F32),
            pltpu.VMEM((NZ, 16, VB), F32),
            pltpu.VMEM((NJ, 16, VB), F32),
            pltpu.VMEM((NX, 16, SQ), F32),
            pltpu.VMEM((NX, 16, SQ), F32),
            pltpu.VMEM((NX, 8, SQ), F32),
            pltpu.VMEM((NJ, 3, 8, 128), F32),
            pltpu.VMEM((NJ, 3, 8, 128), F32),
            pltpu.VMEM((NZ, 3, 8, 128), F32),
            pltpu.VMEM((NJ, 8, 128), F32),
            dma((chunks,)),
            dma((tchunks,)),
            dma((2, NZ)),
            dma((2, NJ)),
            dma((2, NX)),
            dma((2, NJ)),
            dma((2, NZ)),
            dma((2, NJ)),
            dma((2, NX)),
            dma((2, NX)),
            dma((2, NJ)),
            dma((2, NZ)),
            dma((2, NJ)),
        ],
        compiler_params=pltpu.CompilerParams(
            collective_id=0, has_side_effects=True, vmem_limit_bytes=60 * 1024 * 1024
        ),
    )(
        geno,
        test_geno,
        allele_pct.reshape(1, V),
        test_pct.reshape(1, TV),
        exposure.reshape(RP, 128),
        perm,
        var_comp,
        solution,
        resid,
        direction,
    )


def solution(mesh):
    samp, var = mesh.shape["samp"], mesh.shape["var"]
    near = 8 if samp == 32 else samp // 2

    def whole(geno, *rest):
        dims = (samp // near, near, var, float(geno.shape[1]))
        return jax.shard_map(
            functools.partial(local, dims),
            mesh=mesh,
            in_specs=(
                P("samp", "var"),
                P("var"),
                P("samp", "var"),
                P("var"),
                P("samp"),
                P(None, "samp"),
                P(),
                P(None, "samp"),
                P(None, "samp"),
                P(None, "samp"),
            ),
            out_specs=(P(None, "samp"), P(None, "samp"), P(None, "samp"), P(None, "var")),
            check_vma=False,
        )(geno, *rest)

    return whole
```

```python
import functools

import jax
import jax.numpy as jnp
from jax import lax
from jax.experimental import pallas as pl
from jax.experimental.pallas import tpu as pltpu
from jax.sharding import PartitionSpec as P

MESH = pl.DeviceIdType.MESH
F32 = jnp.float32
BF16 = jnp.bfloat16


def log2(n):
    return n.bit_length() - 1


def split3(value):
    high = value.astype(BF16)
    rest = value - high.astype(F32)
    mid = rest.astype(BF16)
    low = (rest - mid.astype(F32)).astype(BF16)
    return high, mid, low


def sum3(value):
    rows = value.shape[0] // 3
    return value[:rows] + value[rows : 2 * rows] + value[2 * rows :]


def kernel(
    dims,
    geno_hbm, tgeno_hbm, pct_hbm, tpct_hbm, expo_hbm, perm_hbm, vc_hbm, sol_hbm, res_hbm, dir_hbm,
    osol_ref, ores_ref, odir_ref, oassoc_ref,
    vc_ref, expo_ref, perm_ref, pct_ref, tpct_ref, sol_ref, res_ref, dir_ref,
    graw, traw, gbf, tbf, table, tparts, shuf, parts, lefts, squares, acc,
    psend, precv, pz, pall, asend, arecv, irecv, isend, fsend, frecv, fz, fall,
    isem, gsem, tsem, sem_ez, sem_ej, sem_sh, sem_p, sem_pz, sem_pa, sem_a, sem_im, sem_f, sem_fz, sem_fa,
):
    NZ, NJ, NX, scale_rows = dims
    samp = lax.axis_index("samp")
    x = lax.axis_index("var")
    z = samp // NJ
    j = samp % NJ
    core = j % 2
    pair = j - core
    SP = dir_ref.shape[1]
    V = pct_ref.shape[1]
    TV = tpct_ref.shape[1]
    RP = SP // 128
    VB = V // NJ
    SQ = SP // NX
    W = min(SQ, 256)
    chunks = graw.shape[0]
    crows = graw.shape[1]
    tchunks = traw.shape[0]
    trows = traw.shape[1]

    reads = [
        pltpu.make_async_copy(src, dst, isem.at[i])
        for i, (src, dst) in enumerate((
            (expo_hbm, expo_ref), (pct_hbm, pct_ref), (perm_hbm, perm_ref), (dir_hbm, dir_ref),
            (res_hbm, res_ref), (tpct_hbm, tpct_ref), (sol_hbm, sol_ref), (vc_hbm, vc_ref),
        ))
    ]
    reads[0].start()

    def gread(i):
        return pltpu.make_async_copy(geno_hbm.at[pl.ds(i * crows, crows), :], graw.at[i], gsem.at[i])

    def tread(i):
        return pltpu.make_async_copy(tgeno_hbm.at[pl.ds(i * trows, trows), :], traw.at[i], tsem.at[i])

    def to_j(peer):
        return {"samp": z * NJ + peer}

    def to_z(peer):
        return {"samp": peer * NJ + j}

    def to_x(peer):
        return {"var": peer}

    groups = {"j": (j, NJ, to_j), "z": (z, NZ, to_z), "x": (x, NX, to_x)}

    def each_peer(group, body):
        me, count, _ = groups[group]

        def step(t, carry):
            off = count // 2 + ((t + 1) // 2) * (2 * (t % 2) - 1)
            body((me + off) % count)
            return carry

        lax.fori_loop(0, count - 1, step, 0)

    def push(group, src, dst, sem, peer):
        me, _, place = groups[group]
        pltpu.make_async_remote_copy(
            src_ref=src, dst_ref=dst, send_sem=sem.at[0, peer], recv_sem=sem.at[1, me],
            device_id=place(peer), device_id_type=MESH,
        ).start()

    def arrived_one(group, dst, sem, peer):
        place = groups[group][2]
        pltpu.make_async_remote_copy(
            src_ref=dst, dst_ref=dst, send_sem=sem.at[0, peer], recv_sem=sem.at[1, peer],
            device_id=place(peer), device_id_type=MESH,
        ).wait_recv()

    def arrived(group, dst_of, sem):
        each_peer(group, lambda peer: arrived_one(group, dst_of(peer), sem, peer))

    def sent(group, src_of, sem):
        place = groups[group][2]

        def one(peer):
            pltpu.make_async_remote_copy(
                src_ref=src_of(peer), dst_ref=src_of(peer), send_sem=sem.at[0, peer], recv_sem=sem.at[1, peer],
                device_id=place(peer), device_id_type=MESH,
            ).wait_send()

        each_peer(group, one)

    barrier = pltpu.get_barrier_semaphore()
    for group in ("j", "z", "x"):
        place = groups[group][2]
        each_peer(
            group,
            lambda peer, place=place: pl.semaphore_signal(barrier, inc=1, device_id=place(peer), device_id_type=MESH),
        )
    for copy in reads[1:]:
        copy.start()
    for i in range(chunks):
        gread(i).start()
    for i in range(tchunks):
        tread(i).start()
    reads[0].wait()
    pl.semaphore_wait(barrier, NJ + NZ + NX - 3)

    each_peer("z", lambda peer: push("z", expo_ref, table.at[core, z], sem_ez, peer))
    table[core, z] = expo_ref[...]

    reads[1].wait()
    reads[5].wait()
    pct = pct_ref[...].astype(F32)
    tpct = tpct_ref[...].astype(F32)

    def convert(i, carry):
        gread(i).wait()
        block = 32

        def rows(r, carry):
            start = pl.multiple_of(r * block, block)
            codes = graw[i, pl.ds(start, block), :].astype(F32)
            gbf[pl.ds(pl.multiple_of(i * crows + start, block), block), :] = (codes * 50.0 - pct).astype(BF16)
            return carry

        return lax.fori_loop(0, crows // block, rows, carry)

    def tconvert(i, carry):
        tread(i).wait()
        block = 64

        def rows(r, carry):
            start = pl.multiple_of(r * block, block)
            codes = traw[i, pl.ds(start, block), :].astype(F32)
            tbf[pl.ds(pl.multiple_of(i * trows + start, block), block), :] = (codes * 50.0 - tpct).astype(BF16)
            return carry

        return lax.fori_loop(0, trows // block, rows, carry)

    half = 3 * chunks // 8
    lax.fori_loop(0, half, convert, 0)

    arrived("z", lambda peer: table.at[core, peer], sem_ez)
    each_peer("j", lambda peer: push("j", table.at[core], table.at[(j - (peer - peer % 2) + NJ) % NJ], sem_ej, peer))

    lax.fori_loop(half, chunks, convert, 0)
    freq = pct / 100.0
    square = 1.0 / (2.0 * freq * (1.0 - freq)) / 2500.0
    for i in range(NJ):
        squares[i] = square[:, i * VB : (i + 1) * VB]
    for i in (2, 3, 4, 6, 7):
        reads[i].wait()

    rows_half = NJ * NZ * RP // 2
    index = perm_ref[:, pl.ds(pl.multiple_of(x * SQ, SQ), SQ)]
    row_z = index >> log2(SP * NJ)
    row_j = ((index >> log2(SP)) - pair) & (NJ - 1)
    row_r = (index >> 7) & (RP - 1)
    row_of = (row_j * NZ + row_z) * RP + row_r
    lane_of = index & 127
    for h in range(2):
        for place in range(h * NJ // 2, (h + 1) * NJ // 2):

            def block_here(place=place):
                arrived_one("j", table.at[place], sem_ej, (pair + place) % NJ)

            if place < 2:
                pl.when(core != place)(block_here)
            else:
                block_here()
        flat = table[h * NJ // 2 : (h + 1) * NJ // 2].reshape(rows_half, 128)
        high, mid, low = split3(flat.T)
        tparts[0:128, :] = high
        tparts[128:256, :] = mid
        tparts[256:384, :] = low
        for c in range(SQ // W):
            cols = slice(c * W, (c + 1) * W)
            for b in range(8):
                hit = lax.broadcasted_iota(jnp.int32, (rows_half, W), 0) == row_of[b : b + 1, cols] - h * rows_half
                onehot = jnp.where(hit, 1.0, 0.0).astype(BF16)
                picked = sum3(jnp.dot(tparts[...], onehot, preferred_element_type=F32))
                lane_hit = lax.broadcasted_iota(jnp.int32, (128, W), 0) == lane_of[b : b + 1, cols]
                found = jnp.sum(jnp.where(lane_hit, picked, 0.0), axis=0, keepdims=True)
                if h == 0:
                    shuf[x, c, b : b + 1] = found
                else:
                    shuf[x, c, b : b + 1] = shuf[x, c, b : b + 1] + found
            if h == 1:
                each_peer("x", lambda peer, c=c: push("x", shuf.at[x, c], shuf.at[x, c], sem_sh.at[c], peer))

    lax.fori_loop(0, tchunks, tconvert, 0)
    for c in range(SQ // W):
        arrived("x", lambda peer, c=c: shuf.at[peer, c], sem_sh.at[c])

    def stacked(value_of, q):
        for c in range(SQ // W):
            value = value_of(q * SQ + c * W)
            parts_of = split3(jnp.concatenate([value, shuf[q, c] * value], axis=0))
            for k, part in enumerate(parts_of):
                parts[16 * k : 16 * k + 16, q * SQ + c * W : q * SQ + (c + 1) * W] = part

    for q in range(NX):
        stacked(lambda start: dir_ref[:, start : start + W], q)

    def product(block):
        cols = pl.ds(pl.multiple_of(block * VB, VB), VB)
        return sum3(jnp.dot(parts[...], gbf[:, cols], preferred_element_type=F32))

    def product_step(peer):
        psend[peer] = product(peer)
        push("j", psend.at[peer], precv.at[j], sem_p, peer)

    each_peer("j", product_step)
    precv[j] = product(j)

    for q in range(NX):
        stacked(lambda start: res_ref[:, start : start + W], q)
    apart = sum3(jnp.dot(parts[...], tbf[...], preferred_element_type=F32))
    quarters = TV // 128
    for i in range(NJ):
        h, q = divmod(i, quarters)
        asend[i] = apart[8 * h : 8 * h + 8, 128 * q : 128 * q + 128]

    arrived("j", lambda peer: precv.at[peer], sem_p)
    total = precv[0]
    for i in range(1, NJ):
        total = total + precv[i]
    pz[z] = total
    each_peer("z", lambda peer: push("z", pz.at[z], pz.at[z], sem_pz, peer))
    each_peer("j", lambda peer: push("j", asend.at[peer], arecv.at[j], sem_a, peer))
    arecv[j] = asend[j]
    arrived("z", lambda peer: pz.at[peer], sem_pz)
    total = pz[0]
    for i in range(1, NZ):
        total = total + pz[i]
    pall[j] = total
    each_peer("j", lambda peer: push("j", pall.at[j], pall.at[j], sem_pa, peer))

    def halves(first, place):
        for k in range(2):
            block = first + k
            for i, part in enumerate(split3(pall[block] * squares[block])):
                lefts[place, 16 * i : 16 * i + 16, k * VB : (k + 1) * VB] = part

    def against(place, rows, first):
        cols = pl.ds(pl.multiple_of(first * VB, 2 * VB), 2 * VB)
        return lax.dot_general(lefts[place], gbf[rows, cols], (((1,), (1,)), ((), ())), preferred_element_type=F32)

    other = pair + 1 - core
    arrived_one("j", pall.at[other], sem_pa, other)
    halves(pair, 0)
    acc[...] = sum3(against(0, slice(0, SP), pair))
    firsts = [(pair + 2 * k) % NJ for k in range(1, NJ // 2)]
    for first in firsts:
        for k in range(2):
            arrived_one("j", pall.at[first + k], sem_pa, first + k)
    for k, first in enumerate(firsts):
        halves(first, k + 1)

    def part_step(q, carry):
        rows = pl.ds(pl.multiple_of(q * SQ, SQ), SQ)
        value = acc[:, rows]
        if firsts:
            total = against(1, rows, firsts[0])
            for k in range(1, len(firsts)):
                total = total + against(k + 1, rows, firsts[k])
            value = value + sum3(total)
        for c in range(SQ // W):
            cols = slice(c * W, (c + 1) * W)
            isend[q, :, cols] = (
                vc_ref[1] * value[0:8, cols] + vc_ref[2] * shuf[q, c] * value[8:16, cols]
            ) * (1.0 / scale_rows)
        each_peer("x", lambda peer: push("x", isend.at[q], irecv.at[x, q], sem_im.at[q], peer))
        irecv[x, q] = isend[q]
        return carry

    lax.fori_loop(0, NX, part_step, 0)

    sent("z", lambda peer: expo_ref, sem_ez)
    sent("j", lambda peer: table.at[core], sem_ej)
    for c in range(SQ // W):
        sent("x", lambda peer, c=c: shuf.at[x, c], sem_sh.at[c])
    sent("j", lambda peer: psend.at[peer], sem_p)
    sent("z", lambda peer: pz.at[z], sem_pz)
    sent("j", lambda peer: pall.at[j], sem_pa)
    sent("j", lambda peer: asend.at[peer], sem_a)
    arrived("j", lambda peer: arecv.at[peer], sem_a)
    asum = arecv[0]
    for i in range(1, NJ):
        asum = asum + arecv[i]
    sums = [jnp.zeros((8, 1), F32) for _ in range(4)]
    bpart = None
    images = []
    for q in range(NX):
        cols = slice(q * SQ, (q + 1) * SQ)
        arrived("x", lambda peer, q=q: irecv.at[peer, q], sem_im.at[q])
        image = irecv[0, q]
        for i in range(1, NX):
            image = image + irecv[i, q]
        d, r = dir_ref[:, cols], res_ref[:, cols]
        image = vc_ref[0] * d + image
        images.append(image)
        stacked(lambda start, q=q, image=image: image[:, start - q * SQ : start - q * SQ + W], q)
        value = sum3(jnp.dot(parts[:, cols], tbf[cols, :], preferred_element_type=F32))
        bpart = value if bpart is None else bpart + value
        for k, term in enumerate((r * r, d * image, r * image, image * image)):
            sums[k] = sums[k] + jnp.sum(term, axis=1, keepdims=True)
    lane = lax.broadcasted_iota(jnp.int32, (8, 128), 1)
    scalars = jnp.where(lane == 0, sums[0], jnp.where(lane == 1, sums[1], jnp.where(lane == 2, sums[2], sums[3])))
    for i in range(NJ):
        h, q = divmod(i, quarters)
        fsend[i, 0] = bpart[8 * h : 8 * h + 8, 128 * q : 128 * q + 128]
        fsend[i, 1] = scalars
    each_peer("j", lambda peer: push("j", fsend.at[peer], frecv.at[j], sem_f, peer))
    frecv[j] = fsend[j]
    for q in range(NX):
        sent("x", lambda peer, q=q: isend.at[q], sem_im.at[q])
    for q in range(NX):
        isend[q] = images[q]
    arrived("j", lambda peer: frecv.at[peer], sem_f)
    total = frecv[0]
    for i in range(1, NJ):
        total = total + frecv[i]
    fz[z, 0] = asum
    fz[z, 1] = total[0]
    fz[z, 2] = total[1]
    each_peer("z", lambda peer: push("z", fz.at[z], fz.at[z], sem_fz, peer))
    sent("j", lambda peer: fsend.at[peer], sem_f)
    arrived("z", lambda peer: fz.at[peer], sem_fz)
    total = fz[0]
    for i in range(1, NZ):
        total = total + fz[i]
    norm_now = total[2][:, 0:1]
    curvature = total[2][:, 1:2]
    alpha = norm_now / curvature
    fall[j] = total[0] - alpha * total[1]
    each_peer("j", lambda peer: push("j", fall.at[j], fall.at[j], sem_fa, peer))

    norm_next = norm_now - 2.0 * alpha * total[2][:, 2:3] + alpha * alpha * total[2][:, 3:4]
    beta = norm_next / norm_now
    for q in range(NX):
        cols = slice(q * SQ, (q + 1) * SQ)
        d = dir_ref[:, cols]
        new_res = res_ref[:, cols] - alpha * isend[q]
        osol_ref[:, cols] = sol_ref[:, cols] + alpha * d
        ores_ref[:, cols] = new_res
        odir_ref[:, cols] = new_res + beta * d
    sent("z", lambda peer: fz.at[z], sem_fz)

    tfreq = tpct / 100.0
    root = float(NZ * NJ * SP) ** 0.5 * 50.0
    tscale = lax.rsqrt(2.0 * tfreq * (1.0 - tfreq)) / root
    arrived("j", lambda peer: fall.at[peer], sem_fa)
    for i in range(NJ):
        h, q = divmod(i, quarters)
        cols = slice(128 * q, 128 * q + 128)
        oassoc_ref[8 * h : 8 * h + 8, cols] = fall[i] * tscale[:, cols]
    sent("j", lambda peer: fall.at[j], sem_fa)


def local(dims, geno, allele_pct, test_geno, test_pct, exposure, perm, var_comp, solution, resid, direction):
    NZ, NJ, NX, _ = dims
    SP, V = geno.shape
    TV = test_geno.shape[1]
    RP, VB, SQ = SP // 128, V // NJ, SP // NX
    W = min(SQ, 256)
    chunks, tchunks = 8, 2
    vmem = pl.BlockSpec(memory_space=pltpu.VMEM)
    hbm = pl.BlockSpec(memory_space=pltpu.HBM)
    dma = pltpu.SemaphoreType.DMA
    rhs = jax.ShapeDtypeStruct((8, SP), F32)
    outs = (rhs, rhs, rhs, jax.ShapeDtypeStruct((16, TV), F32))
    results = pl.pallas_call(
        functools.partial(kernel, dims),
        out_shape=outs,
        in_specs=[hbm] * 10,
        out_specs=(vmem, vmem, vmem, vmem),
        scratch_shapes=[
            pltpu.SMEM((3,), F32),
            pltpu.VMEM((RP, 128), F32),
            pltpu.VMEM((8, SP), jnp.int32),
            pltpu.VMEM((1, V), jnp.int32),
            pltpu.VMEM((1, TV), jnp.int32),
            pltpu.VMEM((8, SP), F32),
            pltpu.VMEM((8, SP), F32),
            pltpu.VMEM((8, SP), F32),
            pltpu.VMEM((chunks, SP // chunks, V), jnp.int32),
            pltpu.VMEM((tchunks, SP // tchunks, TV), jnp.int32),
            pltpu.VMEM((SP, V), BF16),
            pltpu.VMEM((SP, TV), BF16),
            pltpu.VMEM((NJ, NZ, RP, 128), F32),
            pltpu.VMEM((384, NJ * NZ * RP // 2), BF16),
            pltpu.VMEM((NX, SQ // W, 8, W), F32),
            pltpu.VMEM((48, max(SP, V)), BF16),
            pltpu.VMEM((NJ // 2, 48, 2 * VB), BF16),
            pltpu.VMEM((NJ, 1, VB), F32),
            pltpu.VMEM((16, SP), F32),
            pltpu.VMEM((NJ, 16, VB), F32),
            pltpu.VMEM((NJ, 16, VB), F32),
            pltpu.VMEM((NZ, 16, VB), F32),
            pltpu.VMEM((NJ, 16, VB), F32),
            pltpu.VMEM((NJ, 8, 128), F32),
            pltpu.VMEM((NJ, 8, 128), F32),
            pltpu.VMEM((NX, NX, 8, SQ), F32),
            pltpu.VMEM((NX, 8, SQ), F32),
            pltpu.VMEM((NJ, 2, 8, 128), F32),
            pltpu.VMEM((NJ, 2, 8, 128), F32),
            pltpu.VMEM((NZ, 3, 8, 128), F32),
            pltpu.VMEM((NJ, 8, 128), F32),
            dma((8,)),
            dma((chunks,)),
            dma((tchunks,)),
            dma((2, NZ)),
            dma((2, NJ)),
            dma((SQ // W, 2, NX)),
            dma((2, NJ)),
            dma((2, NZ)),
            dma((2, NJ)),
            dma((2, NJ)),
            dma((NX, 2, NX)),
            dma((2, NJ)),
            dma((2, NZ)),
            dma((2, NJ)),
        ],
        compiler_params=pltpu.CompilerParams(
            collective_id=0, has_side_effects=True, vmem_limit_bytes=40 * 1024 * 1024
        ),
    )(
        *(
            pltpu.with_memory_space_constraint(value, pltpu.HBM)
            for value in (
                geno,
                test_geno,
                allele_pct.reshape(1, V),
                test_pct.reshape(1, TV),
                exposure.reshape(RP, 128),
                perm,
                var_comp,
                solution,
                resid,
                direction,
            )
        )
    )
    return pl.pallas_call(
        hand_over,
        out_shape=outs,
        in_specs=[vmem] * 4,
        out_specs=(vmem,) * 4,
        compiler_params=pltpu.CompilerParams(vmem_limit_bytes=2 * 1024 * 1024),
    )(*results)


def hand_over(*refs):
    for source, target in zip(refs[:4], refs[4:]):
        target[...] = source[...]


def solution(mesh):
    samp, var = mesh.shape["samp"], mesh.shape["var"]
    near = 8 if samp == 32 else samp // 2

    def whole(geno, *rest):
        dims = (samp // near, near, var, float(geno.shape[1]))
        return jax.shard_map(
            functools.partial(local, dims),
            mesh=mesh,
            in_specs=(
                P("samp", "var"),
                P("var"),
                P("samp", "var"),
                P("var"),
                P("samp"),
                P(None, "samp"),
                P(),
                P(None, "samp"),
                P(None, "samp"),
                P(None, "samp"),
            ),
            out_specs=(P(None, "samp"), P(None, "samp"), P(None, "samp"), P(None, "var")),
            check_vma=False,
        )(geno, *rest)

    return whole
```

```python
import functools

import jax
import jax.numpy as jnp
from jax import lax
from jax.experimental import pallas as pl
from jax.experimental.pallas import tpu as pltpu
from jax.sharding import PartitionSpec as P

MESH = pl.DeviceIdType.MESH
F32 = jnp.float32
BF16 = jnp.bfloat16


def log2(n):
    return n.bit_length() - 1


def split3(value):
    high = value.astype(BF16)
    rest = value - high.astype(F32)
    mid = rest.astype(BF16)
    low = (rest - mid.astype(F32)).astype(BF16)
    return high, mid, low


def sum3(value):
    rows = value.shape[0] // 3
    return value[:rows] + value[rows : 2 * rows] + value[2 * rows :]


def kernel(
    dims,
    geno_hbm, tgeno_hbm, pct_hbm, tpct_hbm, expo_hbm, perm_hbm, vc_hbm, sol_hbm, res_hbm, dir_hbm,
    osol_ref, ores_ref, odir_ref, oassoc_ref,
    vc_ref, perm_ref, pct_ref, tpct_ref, sol_ref, res_ref, dir_ref,
    graw, traw, gbf, tbf, table, tparts, row_of, lane_of, shuf, parts, lefts, squares, acc, image_ref, apart, bpart,
    psend, precv, pz, pall, asend, arecv, aall, irecv, isend, fsend, frecv, fall, sums_z,
    isem, gsem, tsem, sem_ez, sem_ej, sem_sh, sem_p, sem_pz, sem_pa, sem_a, sem_aa, sem_im, sem_f, sem_fa, sem_sz,
):
    NZ, NJ, NX, scale_rows = dims
    NY, NS = NJ // 2, NZ * NJ
    samp = lax.axis_index("samp")
    x = lax.axis_index("var")
    z = samp // NJ
    j = samp % NJ
    core = j % 2
    pair = j - core
    SP = dir_ref.shape[1]
    V = pct_ref.shape[1]
    TV = tpct_ref.shape[1]
    RP = SP // 128
    VB = V // NJ
    SQ = SP // NX
    W = min(SQ, 256)
    CW = SQ // W
    quarters = TV // 128
    chunks = graw.shape[0]
    crows = graw.shape[1]
    tchunks = traw.shape[0]
    trows = traw.shape[1]

    def loop(count, body):
        def step(i, carry):
            body(i)
            return carry

        lax.fori_loop(0, count, step, 0)

    def block(i, size):
        return pl.ds(pl.multiple_of(i * size, size), size)

    reads = [
        pltpu.make_async_copy(src, dst, isem.at[i])
        for i, (src, dst) in enumerate((
            (expo_hbm, table.at[core, z]), (pct_hbm, pct_ref), (perm_hbm, perm_ref), (dir_hbm, dir_ref),
            (res_hbm, res_ref), (tpct_hbm, tpct_ref), (sol_hbm, sol_ref), (vc_hbm, vc_ref),
        ))
    ]

    def gread(i):
        return pltpu.make_async_copy(geno_hbm.at[pl.ds(i * crows, crows), :], graw.at[i], gsem.at[i])

    def tread(i):
        return pltpu.make_async_copy(tgeno_hbm.at[pl.ds(i * trows, trows), :], traw.at[i], tsem.at[i])

    def outward(t, count):
        return (count // 2 + ((t + 1) // 2) * (2 * (t % 2) - 1)) % count

    def to_near(peer):
        return {"samp": z * NJ + peer}

    def nth_near(t):
        side = (core + t % 2 + t // (NJ - 2)) % 2
        return (pair + 2 * outward(t // 2, NY)) % NJ + side

    def to_z(peer):
        return {"samp": peer * NJ + j}

    def nth_z(t):
        return (z + outward(t, NZ)) % NZ

    def to_x(peer):
        return {"var": peer}

    def nth_x(t):
        return (x + outward(t, NX)) % NX

    def to_any(peer):
        return {"samp": peer}

    def nth_any(t):
        return (samp + NS // 2) % NS

    near = (NJ, nth_near, to_near)
    over_z = (NZ, nth_z, to_z)
    over_x = (NX, nth_x, to_x)
    everyone = (NS, nth_any, to_any)

    def each_peer(group, body, rolled=False):
        count, nth, _ = group
        if group is not everyone:
            if rolled:
                loop(count - 1, lambda t: body(nth(t)))
            else:
                for t in range(count - 1):
                    body(nth(t))
            return

        def plane(t):
            first = (z + outward(t, NZ)) % NZ * NJ
            for k in range(NY):
                chip = first + (pair + 2 * outward(k, NY)) % NJ
                body(chip + 1 - core)
                if k < NY - 1:
                    body(chip + core)
                else:
                    pl.when(t < NZ - 1)(lambda chip=chip: body(chip + core))

        loop(NZ, plane)

    def push(group, src, dst, sem, peer, arrival=1):
        pltpu.make_async_remote_copy(
            src_ref=src, dst_ref=dst, send_sem=sem.at[0], recv_sem=sem.at[arrival],
            device_id=group[2](peer), device_id_type=MESH,
        ).start()

    def described(group, like, sem, arrival):
        return pltpu.make_async_remote_copy(
            src_ref=like, dst_ref=like, send_sem=sem.at[0], recv_sem=sem.at[arrival],
            device_id=group[2](group[1](0)), device_id_type=MESH,
        )

    def arrived(group, like, sem, arrival=1):
        described(group, like, sem, arrival).wait_recv()

    def sent(group, like, sem):
        described(group, like, sem, 1).wait_send()

    barrier = pltpu.get_barrier_semaphore()
    reads[0].start()
    for group in (near, over_z, over_x):
        each_peer(
            group,
            lambda peer, group=group: pl.semaphore_signal(
                barrier, inc=1, device_id=group[2](peer), device_id_type=MESH
            ),
        )
    for copy in reads[1:]:
        copy.start()
    loop(chunks, lambda i: gread(i).start())
    loop(tchunks, lambda i: tread(i).start())
    pl.semaphore_wait(barrier, NJ + NZ + NX - 3)

    each_peer(over_z, lambda peer: push(over_z, expo_hbm, table.at[core, z], sem_ez, peer))

    reads[1].wait()
    reads[5].wait()
    pct = pct_ref[...].astype(F32)
    tpct = tpct_ref[...].astype(F32)

    def convert(i):
        gread(i).wait()

        def rows(r):
            codes = graw[i, block(r, 32), :].astype(F32)
            gbf[block(i * (crows // 32) + r, 32), :] = (codes * 50.0 - pct).astype(BF16)

        loop(crows // 32, rows)

    def tconvert(i):
        tread(i).wait()

        def rows(r):
            codes = traw[i, block(r, 64), :].astype(F32)
            tbf[block(i * (trows // 64) + r, 64), :] = (codes * 50.0 - tpct).astype(BF16)

        loop(trows // 64, rows)

    loop(chunks // 2, convert)

    reads[0].wait()
    arrived(over_z, table.at[0, pl.ds(0, NZ - 1)], sem_ez)

    def share(peer):
        place = (j - (peer - peer % 2) + NJ) % NJ
        push(near, table.at[core], table.at[place], sem_ej, peer, 1 + place // NY)

    each_peer(near, share)

    loop(chunks - chunks // 2, lambda i: convert(chunks // 2 + i))
    freq = pct / 100.0
    square = 1.0 / (2.0 * freq * (1.0 - freq)) / 2500.0
    for i in range(NJ):
        squares[i] = square[:, i * VB : (i + 1) * VB]
    for i in (2, 3, 4, 6, 7):
        reads[i].wait()

    rows_half = NS * RP // 2
    index = perm_ref[:, block(x, SQ)]
    index_z = index >> log2(SP * NJ)
    index_j = ((index >> log2(SP)) - pair) & (NJ - 1)
    index_r = (index >> 7) & (RP - 1)
    row = (index_j * NZ + index_z) * RP + index_r
    for b in range(8):
        row_of[b] = row[b : b + 1]
        lane_of[b] = index[b : b + 1] & 127
    sublane = lax.broadcasted_iota(jnp.int32, (8, W), 0)
    deep = lax.broadcasted_iota(jnp.int32, (rows_half, W), 0)
    lanes = lax.broadcasted_iota(jnp.int32, (128, W), 0)
    for h in range(2):
        arrived(near, table.at[pl.ds(0, NY - 1 + h)], sem_ej, 1 + h)
        flat = table[h * NY : (h + 1) * NY].reshape(rows_half, 128)
        for k, part in enumerate(split3(flat.T)):
            tparts[128 * k : 128 * k + 128, :] = part

        def lookup(c, h=h):
            cols = block(c, W)

            found = jnp.zeros((8, W), F32)
            for b in range(8):
                onehot = jnp.where(deep == row_of[b, :, cols] - h * rows_half, 1.0, 0.0).astype(BF16)
                picked = sum3(jnp.dot(tparts[...], onehot, preferred_element_type=F32))
                value = jnp.sum(jnp.where(lanes == lane_of[b, :, cols], picked, 0.0), axis=0, keepdims=True)
                found = jnp.where(sublane == b, value, found)
            mine = x * CW + c
            if h == 0:
                shuf[mine] = found
            else:
                shuf[mine] = shuf[mine] + found
                each_peer(over_x, lambda peer: push(over_x, shuf.at[mine], shuf.at[mine], sem_sh, peer))

        loop(CW, lookup)

    loop(tchunks, tconvert)
    arrived(over_x, shuf.at[pl.ds(0, CW * (NX - 1))], sem_sh)

    def stack(value, i):
        for k, part in enumerate(split3(jnp.concatenate([value, shuf[i] * value], axis=0))):
            parts[16 * k : 16 * k + 16, block(i, W)] = part

    loop(SP // W, lambda i: stack(dir_ref[:, block(i, W)], i))

    def product(target, place, t):
        target[place] = sum3(jnp.dot(parts[...], gbf[:, block(t, VB)], preferred_element_type=F32))

    def product_step(peer):
        product(psend, peer, peer)
        push(near, psend.at[peer], precv.at[j], sem_p, peer)

    each_peer(near, product_step, rolled=True)
    product(precv, j, j)

    loop(SP // W, lambda i: stack(res_ref[:, block(i, W)], i))
    TW = min(TV, 256)

    def ascore(i):
        cols = block(i, TW)
        apart[:, cols] = sum3(jnp.dot(parts[...], tbf[:, cols], preferred_element_type=F32))

    loop(TV // TW, ascore)
    spots = []
    for i in range(NJ):
        h, q = divmod(i, quarters)
        spots.append((slice(8 * h, 8 * h + 8), slice(128 * q, 128 * q + 128)))
    for i, spot in enumerate(spots):
        asend[i] = apart[spot]

    arrived(near, precv.at[pl.ds(0, NJ - 1)], sem_p)
    total = precv[0]
    for i in range(1, NJ):
        total = total + precv[i]
    pz[z] = total
    each_peer(over_z, lambda peer: push(over_z, pz.at[z], pz.at[z], sem_pz, peer))
    each_peer(near, lambda peer: push(near, asend.at[peer], arecv.at[j], sem_a, peer))
    arecv[j] = asend[j]
    arrived(over_z, pz.at[pl.ds(0, NZ - 1)], sem_pz)
    total = pz[0]
    for i in range(1, NZ):
        total = total + pz[i]
    pall[j] = total

    def share_sum(peer):
        other = (peer - peer % 2 - pair + NJ) % NJ
        push(near, pall.at[j], pall.at[j], sem_pa, peer, 1 + (other + NJ - 1) // NJ)

    each_peer(near, share_sum)

    def halves(first, place):
        for k in range(2):
            for i, part in enumerate(split3(pall[first + k] * squares[first + k])):
                lefts[place, 16 * i : 16 * i + 16, k * VB : (k + 1) * VB] = part

    def against(place, rows, first):
        cols = pl.ds(pl.multiple_of(first * VB, 2 * VB), 2 * VB)
        return lax.dot_general(lefts[place], gbf[rows, cols], (((1,), (1,)), ((), ())), preferred_element_type=F32)

    arrived(near, pall.at[0], sem_pa, 1)
    halves(pair, 0)

    def own_part(q):
        acc[q] = against(0, block(q, SQ), pair)

    loop(NX, own_part)
    arrived(near, arecv.at[pl.ds(0, NJ - 1)], sem_a)
    total = arecv[0]
    for i in range(1, NJ):
        total = total + arecv[i]
    aall[samp] = total
    each_peer(everyone, lambda peer: push(everyone, aall.at[samp], aall.at[samp], sem_aa, peer))
    arrived(near, pall.at[pl.ds(0, NJ - 2)], sem_pa, 2)
    firsts = [(pair + 2 * k) % NJ for k in range(1, NY)]
    loop(NY - 1, lambda k: halves((pair + 2 * (k + 1)) % NJ, k + 1))

    def part_step(q):
        total = acc[q]
        for k, first in enumerate(firsts):
            total = total + against(k + 1, block(q, SQ), first)
        value = sum3(total)
        for c in range(CW):
            cols = slice(c * W, (c + 1) * W)
            isend[q, :, cols] = (
                vc_ref[1] * value[0:8, cols] + vc_ref[2] * shuf[q * CW + c] * value[8:16, cols]
            ) * (1.0 / scale_rows)
        each_peer(over_x, lambda peer: push(over_x, isend.at[q], irecv.at[q, x], sem_im.at[q], peer))
        irecv[q, x] = isend[q]

    loop(NX, part_step)

    sent(over_z, table.at[0, pl.ds(0, NZ - 1)], sem_ez)
    sent(near, table.at[pl.ds(0, NJ - 1)], sem_ej)
    sent(over_x, shuf.at[pl.ds(0, CW * (NX - 1))], sem_sh)
    sent(near, psend.at[pl.ds(0, NJ - 1)], sem_p)
    sent(over_z, pz.at[pl.ds(0, NZ - 1)], sem_pz)
    sent(near, pall.at[pl.ds(0, NJ - 1)], sem_pa)
    sent(near, asend.at[pl.ds(0, NJ - 1)], sem_a)
    sent(everyone, aall.at[pl.ds(0, NS - 1)], sem_aa)
    arrived(everyone, aall.at[pl.ds(0, NS - 1)], sem_aa)
    for i, spot in enumerate(spots):
        total = aall[i]
        for k in range(1, NZ):
            total = total + aall[k * NJ + i]
        apart[spot] = total
    bpart[...] = jnp.zeros_like(bpart)

    def score(q, sums):
        arrived(over_x, irecv.at[q, pl.ds(0, NX - 1)], sem_im.at[q])
        image = irecv[q, 0]
        for i in range(1, NX):
            image = image + irecv[q, i]
        cols = block(q, SQ)
        d, r = dir_ref[:, cols], res_ref[:, cols]
        image = vc_ref[0] * d + image
        image_ref[:, cols] = image
        for c in range(CW):
            stack(image[:, c * W : (c + 1) * W], q * CW + c)
        bpart[...] += sum3(jnp.dot(parts[:, cols], tbf[cols, :], preferred_element_type=F32))
        sums = list(sums)
        for k, term in enumerate((r * r, d * image, r * image, image * image)):
            for c in range(SQ // 128):
                sums[k] = sums[k] + term[:, 128 * c : 128 * c + 128]
        return tuple(sums)

    sums = lax.fori_loop(0, NX, score, (jnp.zeros((8, 128), F32),) * 4)
    lane = lax.broadcasted_iota(jnp.int32, (8, 128), 1) - lax.broadcasted_iota(jnp.int32, (8, 128), 0)
    scalars = jnp.zeros((8, 128), F32)
    for k in range(4):
        scalars = jnp.where(lane == 8 * k, jnp.sum(sums[k], axis=1, keepdims=True), scalars)
    scalars = jnp.broadcast_to(jnp.sum(scalars, axis=0, keepdims=True), (8, 128))
    for i, spot in enumerate(spots):
        fsend[i, 0] = bpart[spot]
        fsend[i, 1] = scalars
    each_peer(near, lambda peer: push(near, fsend.at[peer], frecv.at[j], sem_f, peer))
    frecv[j] = fsend[j]
    for q in range(NX):
        sent(over_x, isend.at[pl.ds(0, NX - 1)], sem_im.at[q])
    arrived(near, frecv.at[pl.ds(0, NJ - 1)], sem_f)
    total = frecv[0]
    for i in range(1, NJ):
        total = total + frecv[i]
    fall[samp] = total[0]
    sums_z[z] = total[1]
    each_peer(everyone, lambda peer: push(everyone, fall.at[samp], fall.at[samp], sem_fa, peer))
    each_peer(over_z, lambda peer: push(over_z, sums_z.at[z], sums_z.at[z], sem_sz, peer))
    arrived(over_z, sums_z.at[pl.ds(0, NZ - 1)], sem_sz)
    row = sums_z[0]
    for i in range(1, NZ):
        row = row + sums_z[i]
    norm_now, curvature, cross, square = (
        jnp.sum(jnp.where(lane == 8 * k, row, 0.0), axis=1, keepdims=True) for k in range(4)
    )
    alpha = norm_now / curvature

    norm_next = norm_now - 2.0 * alpha * cross + alpha * alpha * square
    beta = norm_next / norm_now
    d = dir_ref[...]
    new_res = res_ref[...] - alpha * image_ref[...]
    osol_ref[...] = sol_ref[...] + alpha * d
    ores_ref[...] = new_res
    odir_ref[...] = new_res + beta * d
    sent(near, fsend.at[pl.ds(0, NJ - 1)], sem_f)
    sent(over_z, sums_z.at[pl.ds(0, NZ - 1)], sem_sz)

    tfreq = tpct / 100.0
    root = float(NS * SP) ** 0.5 * 50.0
    tscale = lax.rsqrt(2.0 * tfreq * (1.0 - tfreq)) / root
    arrived(everyone, fall.at[pl.ds(0, NS - 1)], sem_fa)
    for i, spot in enumerate(spots):
        total = fall[i]
        for k in range(1, NZ):
            total = total + fall[k * NJ + i]
        oassoc_ref[spot] = (apart[spot] - alpha * total) * tscale[:, spot[1]]
    sent(everyone, fall.at[pl.ds(0, NS - 1)], sem_fa)


def local(dims, geno, allele_pct, test_geno, test_pct, exposure, perm, var_comp, solution, resid, direction):
    NZ, NJ, NX, _ = dims
    SP, V = geno.shape
    TV = test_geno.shape[1]
    RP, VB, SQ = SP // 128, V // NJ, SP // NX
    W = min(SQ, 256)
    chunks, tchunks = 4, 1
    NS = NZ * NJ
    vmem = pl.BlockSpec(memory_space=pltpu.VMEM)
    hbm = pl.BlockSpec(memory_space=pltpu.HBM)
    dma = pltpu.SemaphoreType.DMA
    rhs = jax.ShapeDtypeStruct((8, SP), F32)
    outs = (rhs, rhs, rhs, jax.ShapeDtypeStruct((16, TV), F32))
    results = pl.pallas_call(
        functools.partial(kernel, dims),
        out_shape=outs,
        in_specs=[hbm] * 10,
        out_specs=(vmem, vmem, vmem, vmem),
        scratch_shapes=[
            pltpu.SMEM((3,), F32),
            pltpu.VMEM((8, SP), jnp.int32),
            pltpu.VMEM((1, V), jnp.int32),
            pltpu.VMEM((1, TV), jnp.int32),
            pltpu.VMEM((8, SP), F32),
            pltpu.VMEM((8, SP), F32),
            pltpu.VMEM((8, SP), F32),
            pltpu.VMEM((chunks, SP // chunks, V), jnp.int32),
            pltpu.VMEM((tchunks, SP // tchunks, TV), jnp.int32),
            pltpu.VMEM((SP, V), BF16),
            pltpu.VMEM((SP, TV), BF16),
            pltpu.VMEM((NJ, NZ, RP, 128), F32),
            pltpu.VMEM((384, NS * RP // 2), BF16),
            pltpu.VMEM((8, 1, SQ), jnp.int32),
            pltpu.VMEM((8, 1, SQ), jnp.int32),
            pltpu.VMEM((SP // W, 8, W), F32),
            pltpu.VMEM((48, SP), BF16),
            pltpu.VMEM((NJ // 2, 48, 2 * VB), BF16),
            pltpu.VMEM((NJ, 1, VB), F32),
            pltpu.VMEM((NX, 48, SQ), F32),
            pltpu.VMEM((8, SP), F32),
            pltpu.VMEM((16, TV), F32),
            pltpu.VMEM((16, TV), F32),
            pltpu.VMEM((NJ, 16, VB), F32),
            pltpu.VMEM((NJ, 16, VB), F32),
            pltpu.VMEM((NZ, 16, VB), F32),
            pltpu.VMEM((NJ, 16, VB), F32),
            pltpu.VMEM((NJ, 8, 128), F32),
            pltpu.VMEM((NJ, 8, 128), F32),
            pltpu.VMEM((NS, 8, 128), F32),
            pltpu.VMEM((NX, NX, 8, SQ), F32),
            pltpu.VMEM((NX, 8, SQ), F32),
            pltpu.VMEM((NJ, 2, 8, 128), F32),
            pltpu.VMEM((NJ, 2, 8, 128), F32),
            pltpu.VMEM((NS, 8, 128), F32),
            pltpu.VMEM((NZ, 8, 128), F32),
            dma((8,)),
            dma((chunks,)),
            dma((tchunks,)),
            dma((2,)),
            dma((3,)),
            dma((2,)),
            dma((2,)),
            dma((2,)),
            dma((3,)),
            dma((2,)),
            dma((2,)),
            dma((NX, 2)),
            dma((2,)),
            dma((2,)),
            dma((2,)),
        ],
        compiler_params=pltpu.CompilerParams(
            collective_id=0, has_side_effects=True, vmem_limit_bytes=40 * 1024 * 1024
        ),
    )(
        *(
            pltpu.with_memory_space_constraint(value, pltpu.HBM)
            for value in (
                geno,
                test_geno,
                allele_pct.reshape(1, V),
                test_pct.reshape(1, TV),
                exposure.reshape(RP, 128),
                perm,
                var_comp,
                solution,
                resid,
                direction,
            )
        )
    )
    return pl.pallas_call(
        hand_over,
        out_shape=outs,
        in_specs=[vmem] * 4,
        out_specs=(vmem,) * 4,
        compiler_params=pltpu.CompilerParams(vmem_limit_bytes=2 * 1024 * 1024),
    )(*results)


def hand_over(*refs):
    for source, target in zip(refs[:4], refs[4:]):
        target[...] = source[...]


def solution(mesh):
    samp, var = mesh.shape["samp"], mesh.shape["var"]
    near = 8 if samp == 32 else samp // 2

    def whole(geno, *rest):
        dims = (samp // near, near, var, float(geno.shape[1]))
        return jax.shard_map(
            functools.partial(local, dims),
            mesh=mesh,
            in_specs=(
                P("samp", "var"),
                P("var"),
                P("samp", "var"),
                P("var"),
                P("samp"),
                P(None, "samp"),
                P(),
                P(None, "samp"),
                P(None, "samp"),
                P(None, "samp"),
            ),
            out_specs=(P(None, "samp"), P(None, "samp"), P(None, "samp"), P(None, "var")),
            check_vma=False,
        )(geno, *rest)

    return whole
```

```python
import functools

import jax
import jax.numpy as jnp
from jax import lax
from jax.experimental import pallas as pl
from jax.experimental.pallas import tpu as pltpu
from jax.sharding import PartitionSpec as P

MESH = pl.DeviceIdType.MESH
F32 = jnp.float32
BF16 = jnp.bfloat16


def log2(n):
    return n.bit_length() - 1


def split3(value):
    high = value.astype(BF16)
    rest = value - high.astype(F32)
    mid = rest.astype(BF16)
    low = (rest - mid.astype(F32)).astype(BF16)
    return high, mid, low


def sum3(value):
    rows = value.shape[0] // 3
    return value[:rows] + value[rows : 2 * rows] + value[2 * rows :]


def kernel(
    dims,
    geno_hbm, tgeno_hbm, pct_hbm, tpct_hbm, expo_hbm, perm_hbm, vc_hbm, sol_hbm, res_hbm, dir_hbm,
    osol_ref, ores_ref, odir_ref, oassoc_ref,
    vc_ref, perm_ref, pct_ref, tpct_ref, sol_ref, res_ref, dir_ref,
    graw, traw, gbf, tbf, table, tparts, row_of, lane_of, shuf, parts, lefts, squares, pacc, acc, image_ref, apart, bpart,
    psend, precv, pz, pall, asend, arecv, az, aall, irecv, isend, fsend, frecv, fall, sums_z,
    isem, gsem, tsem, sem_ez, sem_ej, sem_sh, sem_p, sem_pz, sem_pa, sem_a, sem_az, sem_aa, sem_im, sem_f, sem_fa, sem_sz,
):
    NZ, NJ, NX, scale_rows = dims
    NY, NS = NJ // 2, NZ * NJ
    samp = lax.axis_index("samp")
    x = lax.axis_index("var")
    z = samp // NJ
    j = samp % NJ
    core = j % 2
    pair = j - core
    y = j // 2
    SP = dir_ref.shape[1]
    V = pct_ref.shape[1]
    TV = tpct_ref.shape[1]
    RP = SP // 128
    VB = V // NJ
    SQ = SP // NX
    W = min(SQ, 256)
    CW = SQ // W
    quarters = TV // 128
    chunks = graw.shape[0]
    crows = graw.shape[1]
    tchunks = traw.shape[0]
    trows = traw.shape[1]

    def loop(count, body):
        def step(i, carry):
            body(i)
            return carry

        lax.fori_loop(0, count, step, 0)

    def block(i, size):
        return pl.ds(pl.multiple_of(i * size, size), size)

    reads = [
        pltpu.make_async_copy(src, dst, isem.at[i])
        for i, (src, dst) in enumerate((
            (expo_hbm, table.at[core]), (pct_hbm, pct_ref), (perm_hbm, perm_ref), (dir_hbm, dir_ref),
            (res_hbm, res_ref), (tpct_hbm, tpct_ref), (sol_hbm, sol_ref), (vc_hbm, vc_ref),
        ))
    ]

    def gread(i):
        return pltpu.make_async_copy(geno_hbm.at[pl.ds(i * crows, crows), :], graw.at[i], gsem.at[i])

    def tread(i):
        return pltpu.make_async_copy(tgeno_hbm.at[pl.ds(i * trows, trows), :], traw.at[i], tsem.at[i])

    def outward(t, count):
        return (count // 2 + ((t + 1) // 2) * (2 * (t % 2) - 1)) % count

    def to_near(peer):
        return {"samp": z * NJ + peer}

    def nth_near(t):
        side = (core + t % 2 + t // (NJ - 2)) % 2
        return (pair + 2 * outward(t // 2, NY)) % NJ + side

    def to_z(peer):
        return {"samp": peer * NJ + j}

    def nth_z(t):
        return (z + outward(t, NZ)) % NZ

    def to_x(peer):
        return {"var": peer}

    def nth_x(t):
        return (x + outward(t, NX)) % NX

    def to_any(peer):
        return {"samp": peer}

    def nth_any(t):
        return (samp + NS // 2) % NS

    def device(dz, dy, side):
        return (z + dz) % NZ * NJ + (y + dy) % NY * 2 + side

    near = (NJ, nth_near, to_near)
    over_z = (NZ, nth_z, to_z)
    over_x = (NX, nth_x, to_x)
    everyone = (NS, nth_any, to_any)

    def each_peer(group, body, rolled=False):
        count, nth, _ = group
        if group is not everyone:
            if rolled:
                loop(count - 1, lambda t: body(nth(t)))
            else:
                for t in range(count - 1):
                    body(nth(t))
            return

        def plane(t):
            first = (z + outward(t, NZ)) % NZ * NJ
            for k in range(NY):
                chip = first + (pair + 2 * outward(k, NY)) % NJ
                body(chip + 1 - core)
                if k < NY - 1:
                    body(chip + core)
                else:
                    pl.when(t < NZ - 1)(lambda chip=chip: body(chip + core))

        loop(NZ, plane)

    def push(group, src, dst, sem, peer, arrival=1):
        pltpu.make_async_remote_copy(
            src_ref=src, dst_ref=dst, send_sem=sem.at[0], recv_sem=sem.at[arrival],
            device_id=group[2](peer), device_id_type=MESH,
        ).start()

    def described(group, like, sem, arrival):
        return pltpu.make_async_remote_copy(
            src_ref=like, dst_ref=like, send_sem=sem.at[0], recv_sem=sem.at[arrival],
            device_id=group[2](group[1](0)), device_id_type=MESH,
        )

    def arrived(group, like, sem, arrival=1):
        described(group, like, sem, arrival).wait_recv()

    def sent(group, like, sem):
        described(group, like, sem, 1).wait_send()

    barrier = pltpu.get_barrier_semaphore()
    reads[0].start()
    for group in (near, over_z, over_x):
        each_peer(
            group,
            lambda peer, group=group: pl.semaphore_signal(
                barrier, inc=1, device_id=group[2](peer), device_id_type=MESH
            ),
        )
    for side in range(2):
        pl.semaphore_signal(barrier, inc=1, device_id=to_any(device(1, 1, side)), device_id_type=MESH)
    for copy in reads[1:]:
        copy.start()
    loop(chunks, lambda i: gread(i).start())
    loop(tchunks, lambda i: tread(i).start())
    pl.semaphore_wait(barrier, NJ + NZ + NX - 1)

    layers = 2 * NY + 3 * core
    each_peer(
        over_z, lambda peer: push(over_z, expo_hbm, table.at[layers + (z - peer + NZ) % NZ - 1], sem_ez, peer)
    )
    each_peer(
        near, lambda peer: push(near, expo_hbm, table.at[(j - (peer - peer % 2) + NJ) % NJ], sem_ej, peer)
    )
    for side in range(2):
        push(everyone, expo_hbm, table.at[14 + core], sem_ej, device(NZ - 1, NY - 1, side))

    reads[1].wait()
    reads[5].wait()
    pct = pct_ref[...].astype(F32)
    tpct = tpct_ref[...].astype(F32)

    def convert(i):
        gread(i).wait()

        def rows(r):
            codes = graw[i, block(r, 32), :].astype(F32)
            gbf[block(i * (crows // 32) + r, 32), :] = (codes * 50.0 - pct).astype(BF16)

        loop(crows // 32, rows)

    def tconvert(i):
        tread(i).wait()

        def rows(r):
            codes = traw[i, block(r, 64), :].astype(F32)
            tbf[block(i * (trows // 64) + r, 64), :] = (codes * 50.0 - tpct).astype(BF16)

        loop(trows // 64, rows)

    loop(chunks // 2, convert)

    reads[0].wait()
    arrived(over_z, table.at[pl.ds(0, NZ - 1)], sem_ez)

    push(near, table.at[pl.ds(layers, 3)], table.at[pl.ds(layers, 3)], sem_ej, pair + 1 - core)
    for dy, skip, start in ((2, 0, 20), (1, 1, 16), (3, 0, 26)):
        size = 3 - skip
        for side in range(2):
            push(
                everyone, table.at[pl.ds(layers + skip, size)], table.at[pl.ds(start + size * core, size)],
                sem_ej, device(0, NY - dy, side), 2,
            )

    loop(chunks - chunks // 2, lambda i: convert(chunks // 2 + i))
    freq = pct / 100.0
    square = 1.0 / (2.0 * freq * (1.0 - freq)) / 2500.0
    for i in range(NJ):
        squares[i] = square[:, i * VB : (i + 1) * VB]
    for i in (2, 3, 4, 6, 7):
        reads[i].wait()

    rows_half = NS * RP // 2
    index = perm_ref[:, block(x, SQ)]
    dz = ((index >> log2(SP * NJ)) - z) & (NZ - 1)
    dy = ((index >> log2(2 * SP)) - y) & (NY - 1)
    side = (index >> log2(SP)) & 1
    early = jnp.where(dz == 0, 2 * dy + side, jnp.where(dy == 0, 7 + 3 * side + dz, 14 + side))
    late = jnp.where(dy == 1, 14 + 2 * side + dz, jnp.where(dy == 2, 19, 25) + 3 * side + dz)
    place = jnp.where((dz == 0) | (dy == 0) | ((dz == 1) & (dy == 1)), early, late)
    row = place * RP + ((index >> 7) & (RP - 1))
    for b in range(8):
        row_of[b] = row[b : b + 1]
        lane_of[b] = index[b : b + 1] & 127
    sublane = lax.broadcasted_iota(jnp.int32, (8, W), 0)
    deep = lax.broadcasted_iota(jnp.int32, (rows_half, W), 0)
    lanes = lax.broadcasted_iota(jnp.int32, (128, W), 0)
    for h in range(2):
        arrived(near, table.at[pl.ds(0, 12 + 4 * h)], sem_ej, 1 + h)
        flat = table[16 * h : 16 * h + 16].reshape(rows_half, 128)
        for k, part in enumerate(split3(flat.T)):
            tparts[128 * k : 128 * k + 128, :] = part

        def lookup(c, h=h):
            cols = block(c, W)

            found = jnp.zeros((8, W), F32)
            for b in range(8):
                onehot = jnp.where(deep == row_of[b, :, cols] - h * rows_half, 1.0, 0.0).astype(BF16)
                picked = sum3(jnp.dot(tparts[...], onehot, preferred_element_type=F32))
                value = jnp.sum(jnp.where(lanes == lane_of[b, :, cols], picked, 0.0), axis=0, keepdims=True)
                found = jnp.where(sublane == b, value, found)
            mine = x * CW + c
            if h == 0:
                shuf[mine] = found
            else:
                shuf[mine] = shuf[mine] + found
                each_peer(over_x, lambda peer: push(over_x, shuf.at[mine], shuf.at[mine], sem_sh, peer))

        loop(CW, lookup)


    def stack(value, i):
        for k, part in enumerate(split3(jnp.concatenate([value, shuf[i] * value], axis=0))):
            parts[16 * k : 16 * k + 16, block(i, W)] = part

    def stack_dir(i):
        stack(dir_ref[:, block(i, W)], i)

    def on_part(q, t):
        return jnp.dot(parts[:, block(q, SQ)], gbf[block(q, SQ), block(t, VB)], preferred_element_type=F32)

    loop(CW, lambda i: stack_dir(x * CW + i))

    def own_products(i):
        for t in (2 * i, 2 * i + 1):
            pacc[t] = on_part(x, t)

    loop(NJ // 2, own_products)
    loop(tchunks, tconvert)
    arrived(over_x, shuf.at[pl.ds(0, CW * (NX - 1))], sem_sh)
    loop(CW * (NX - 1), lambda i: stack_dir((x * CW + CW + i) % (NX * CW)))

    def product(peer):
        total = pacc[peer]
        for k in range(1, NX):
            total = total + on_part((x + k) % NX, peer)
        psend[peer] = sum3(total)

    def give(peer):
        push(near, psend.at[peer], precv.at[j], sem_p, peer)

    def two_products(i):
        product(nth_near(2 * i))
        product(nth_near(2 * i + 1))
        give(nth_near(2 * i))
        pl.when(i < NJ // 2 - 1)(lambda: give(nth_near(2 * i + 1)))

    loop(NJ // 2, two_products)
    precv[j] = psend[j]

    loop(SP // W, lambda i: stack(res_ref[:, block(i, W)], i))
    TW = min(TV, 256)

    def ascore(i):
        cols = block(i, TW)
        apart[:, cols] = sum3(jnp.dot(parts[...], tbf[:, cols], preferred_element_type=F32))

    loop(TV // TW, ascore)
    spots = []
    for i in range(NJ):
        h, q = divmod(i, quarters)
        spots.append((slice(8 * h, 8 * h + 8), slice(128 * q, 128 * q + 128)))
    for i, spot in enumerate(spots):
        asend[i] = apart[spot]

    arrived(near, precv.at[pl.ds(0, NJ - 1)], sem_p)
    total = precv[0]
    for i in range(1, NJ):
        total = total + precv[i]
    pz[z] = total
    each_peer(over_z, lambda peer: push(over_z, pz.at[z], pz.at[z], sem_pz, peer))
    each_peer(near, lambda peer: push(near, asend.at[peer], arecv.at[j], sem_a, peer))
    arecv[j] = asend[j]
    arrived(over_z, pz.at[pl.ds(0, NZ - 1)], sem_pz)
    total = pz[0]
    for i in range(1, NZ):
        total = total + pz[i]
    pall[j] = total

    def share_sum(peer):
        other = (peer - peer % 2 - pair + NJ) % NJ
        push(near, pall.at[j], pall.at[j], sem_pa, peer, 1 + (other + NJ - 1) // NJ)

    each_peer(near, share_sum)

    arrived(near, arecv.at[pl.ds(0, NJ - 1)], sem_a)
    total = arecv[0]
    for i in range(1, NJ):
        total = total + arecv[i]
    az[z] = total
    each_peer(over_z, lambda peer: push(over_z, az.at[z], az.at[z], sem_az, peer))
    def halves(first, place):
        for k in range(2):
            for i, part in enumerate(split3(pall[first + k] * squares[first + k])):
                lefts[place, 16 * i : 16 * i + 16, k * VB : (k + 1) * VB] = part

    def against(place, rows, first):
        cols = pl.ds(pl.multiple_of(first * VB, 2 * VB), 2 * VB)
        return lax.dot_general(lefts[place], gbf[rows, cols], (((1,), (1,)), ((), ())), preferred_element_type=F32)

    arrived(near, pall.at[0], sem_pa, 1)
    halves(pair, 0)

    def own_part(q):
        acc[q] = against(0, block(q, SQ), pair)

    loop(NX, own_part)
    arrived(near, pall.at[pl.ds(0, NJ - 2)], sem_pa, 2)
    firsts = [(pair + 2 * k) % NJ for k in range(1, NY)]
    loop(NY - 1, lambda k: halves((pair + 2 * (k + 1)) % NJ, k + 1))

    def part_step(q):
        total = acc[q]
        for k, first in enumerate(firsts):
            total = total + against(k + 1, block(q, SQ), first)
        value = sum3(total)
        for c in range(CW):
            cols = slice(c * W, (c + 1) * W)
            isend[q, :, cols] = (
                vc_ref[1] * value[0:8, cols] + vc_ref[2] * shuf[q * CW + c] * value[8:16, cols]
            ) * (1.0 / scale_rows)
        each_peer(over_x, lambda peer: push(over_x, isend.at[q], irecv.at[q, x], sem_im.at[q], peer))
        irecv[q, x] = isend[q]

    loop(NX, part_step)

    arrived(over_z, az.at[pl.ds(0, NZ - 1)], sem_az)
    total = az[0]
    for i in range(1, NZ):
        total = total + az[i]
    aall[j] = total
    each_peer(near, lambda peer: push(near, aall.at[j], aall.at[j], sem_aa, peer))
    sent(over_z, table.at[pl.ds(0, NZ - 1)], sem_ez)
    sent(near, table.at[pl.ds(0, 28)], sem_ej)
    sent(over_x, shuf.at[pl.ds(0, CW * (NX - 1))], sem_sh)
    sent(near, psend.at[pl.ds(0, NJ - 1)], sem_p)
    sent(over_z, pz.at[pl.ds(0, NZ - 1)], sem_pz)
    sent(near, pall.at[pl.ds(0, NJ - 1)], sem_pa)
    sent(near, asend.at[pl.ds(0, NJ - 1)], sem_a)
    bpart[...] = jnp.zeros_like(bpart)

    def score(q, sums):
        arrived(over_x, irecv.at[q, pl.ds(0, NX - 1)], sem_im.at[q])
        image = irecv[q, 0]
        for i in range(1, NX):
            image = image + irecv[q, i]
        cols = block(q, SQ)
        d, r = dir_ref[:, cols], res_ref[:, cols]
        image = vc_ref[0] * d + image
        image_ref[:, cols] = image
        for c in range(CW):
            stack(image[:, c * W : (c + 1) * W], q * CW + c)
        bpart[...] += sum3(jnp.dot(parts[:, cols], tbf[cols, :], preferred_element_type=F32))
        sums = list(sums)
        for k, term in enumerate((r * r, d * image, r * image, image * image)):
            for c in range(SQ // 128):
                sums[k] = sums[k] + term[:, 128 * c : 128 * c + 128]
        return tuple(sums)

    sums = lax.fori_loop(0, NX, score, (jnp.zeros((8, 128), F32),) * 4)
    lane = lax.broadcasted_iota(jnp.int32, (8, 128), 1) - lax.broadcasted_iota(jnp.int32, (8, 128), 0)
    scalars = jnp.zeros((8, 128), F32)
    for k in range(4):
        scalars = jnp.where(lane == 8 * k, jnp.sum(sums[k], axis=1, keepdims=True), scalars)
    scalars = jnp.broadcast_to(jnp.sum(scalars, axis=0, keepdims=True), (8, 128))
    for i, spot in enumerate(spots):
        fsend[i, 0] = bpart[spot]
        fsend[i, 1] = scalars
    each_peer(near, lambda peer: push(near, fsend.at[peer], frecv.at[j], sem_f, peer))
    frecv[j] = fsend[j]
    for q in range(NX):
        sent(over_x, isend.at[pl.ds(0, NX - 1)], sem_im.at[q])
    sent(over_z, az.at[pl.ds(0, NZ - 1)], sem_az)
    sent(near, aall.at[pl.ds(0, NJ - 1)], sem_aa)
    arrived(near, aall.at[pl.ds(0, NJ - 1)], sem_aa)
    arrived(near, frecv.at[pl.ds(0, NJ - 1)], sem_f)
    total = frecv[0]
    for i in range(1, NJ):
        total = total + frecv[i]
    fall[samp] = total[0]
    sums_z[z] = total[1]
    each_peer(everyone, lambda peer: push(everyone, fall.at[samp], fall.at[samp], sem_fa, peer))
    each_peer(over_z, lambda peer: push(over_z, sums_z.at[z], sums_z.at[z], sem_sz, peer))
    arrived(over_z, sums_z.at[pl.ds(0, NZ - 1)], sem_sz)
    row = sums_z[0]
    for i in range(1, NZ):
        row = row + sums_z[i]
    norm_now, curvature, cross, square = (
        jnp.sum(jnp.where(lane == 8 * k, row, 0.0), axis=1, keepdims=True) for k in range(4)
    )
    alpha = norm_now / curvature

    norm_next = norm_now - 2.0 * alpha * cross + alpha * alpha * square
    beta = norm_next / norm_now
    d = dir_ref[...]
    new_res = res_ref[...] - alpha * image_ref[...]
    osol_ref[...] = sol_ref[...] + alpha * d
    ores_ref[...] = new_res
    odir_ref[...] = new_res + beta * d
    sent(near, fsend.at[pl.ds(0, NJ - 1)], sem_f)
    sent(over_z, sums_z.at[pl.ds(0, NZ - 1)], sem_sz)

    tfreq = tpct / 100.0
    root = float(NS * SP) ** 0.5 * 50.0
    tscale = lax.rsqrt(2.0 * tfreq * (1.0 - tfreq)) / root
    arrived(everyone, fall.at[pl.ds(0, NS - 1)], sem_fa)
    for i, spot in enumerate(spots):
        total = fall[i]
        for k in range(1, NZ):
            total = total + fall[k * NJ + i]
        oassoc_ref[spot] = (aall[i] - alpha * total) * tscale[:, spot[1]]
    sent(everyone, fall.at[pl.ds(0, NS - 1)], sem_fa)


def local(dims, geno, allele_pct, test_geno, test_pct, exposure, perm, var_comp, solution, resid, direction):
    NZ, NJ, NX, _ = dims
    SP, V = geno.shape
    TV = test_geno.shape[1]
    RP, VB, SQ = SP // 128, V // NJ, SP // NX
    W = min(SQ, 256)
    chunks, tchunks = 4, 1
    NS = NZ * NJ
    vmem = pl.BlockSpec(memory_space=pltpu.VMEM)
    hbm = pl.BlockSpec(memory_space=pltpu.HBM)
    dma = pltpu.SemaphoreType.DMA
    rhs = jax.ShapeDtypeStruct((8, SP), F32)
    outs = (rhs, rhs, rhs, jax.ShapeDtypeStruct((16, TV), F32))
    results = pl.pallas_call(
        functools.partial(kernel, dims),
        out_shape=outs,
        in_specs=[hbm] * 10,
        out_specs=(vmem, vmem, vmem, vmem),
        scratch_shapes=[
            pltpu.SMEM((3,), F32),
            pltpu.VMEM((8, SP), jnp.int32),
            pltpu.VMEM((1, V), jnp.int32),
            pltpu.VMEM((1, TV), jnp.int32),
            pltpu.VMEM((8, SP), F32),
            pltpu.VMEM((8, SP), F32),
            pltpu.VMEM((8, SP), F32),
            pltpu.VMEM((chunks, SP // chunks, V), jnp.int32),
            pltpu.VMEM((tchunks, SP // tchunks, TV), jnp.int32),
            pltpu.VMEM((SP, V), BF16),
            pltpu.VMEM((SP, TV), BF16),
            pltpu.VMEM((NS, RP, 128), F32),
            pltpu.VMEM((384, NS * RP // 2), BF16),
            pltpu.VMEM((8, 1, SQ), jnp.int32),
            pltpu.VMEM((8, 1, SQ), jnp.int32),
            pltpu.VMEM((SP // W, 8, W), F32),
            pltpu.VMEM((48, SP), BF16),
            pltpu.VMEM((NJ // 2, 48, 2 * VB), BF16),
            pltpu.VMEM((NJ, 1, VB), F32),
            pltpu.VMEM((NJ, 48, VB), F32),
            pltpu.VMEM((NX, 48, SQ), F32),
            pltpu.VMEM((8, SP), F32),
            pltpu.VMEM((16, TV), F32),
            pltpu.VMEM((16, TV), F32),
            pltpu.VMEM((NJ, 16, VB), F32),
            pltpu.VMEM((NJ, 16, VB), F32),
            pltpu.VMEM((NZ, 16, VB), F32),
            pltpu.VMEM((NJ, 16, VB), F32),
            pltpu.VMEM((NJ, 8, 128), F32),
            pltpu.VMEM((NJ, 8, 128), F32),
            pltpu.VMEM((NZ, 8, 128), F32),
            pltpu.VMEM((NJ, 8, 128), F32),
            pltpu.VMEM((NX, NX, 8, SQ), F32),
            pltpu.VMEM((NX, 8, SQ), F32),
            pltpu.VMEM((NJ, 2, 8, 128), F32),
            pltpu.VMEM((NJ, 2, 8, 128), F32),
            pltpu.VMEM((NS, 8, 128), F32),
            pltpu.VMEM((NZ, 8, 128), F32),
            dma((8,)),
            dma((chunks,)),
            dma((tchunks,)),
            dma((2,)),
            dma((3,)),
            dma((2,)),
            dma((2,)),
            dma((2,)),
            dma((3,)),
            dma((2,)),
            dma((2,)),
            dma((2,)),
            dma((NX, 2)),
            dma((2,)),
            dma((2,)),
            dma((2,)),
        ],
        compiler_params=pltpu.CompilerParams(
            collective_id=0, has_side_effects=True, vmem_limit_bytes=40 * 1024 * 1024
        ),
    )(
        *(
            pltpu.with_memory_space_constraint(value, pltpu.HBM)
            for value in (
                geno,
                test_geno,
                allele_pct.reshape(1, V),
                test_pct.reshape(1, TV),
                exposure.reshape(RP, 128),
                perm,
                var_comp,
                solution,
                resid,
                direction,
            )
        )
    )
    return pl.pallas_call(
        hand_over,
        out_shape=outs,
        in_specs=[vmem] * 4,
        out_specs=(vmem,) * 4,
        compiler_params=pltpu.CompilerParams(vmem_limit_bytes=2 * 1024 * 1024),
    )(*results)


def hand_over(*refs):
    for source, target in zip(refs[:4], refs[4:]):
        target[...] = source[...]


def solution(mesh):
    samp, var = mesh.shape["samp"], mesh.shape["var"]
    near = 8 if samp == 32 else samp // 2

    def whole(geno, *rest):
        dims = (samp // near, near, var, float(geno.shape[1]))
        return jax.shard_map(
            functools.partial(local, dims),
            mesh=mesh,
            in_specs=(
                P("samp", "var"),
                P("var"),
                P("samp", "var"),
                P("var"),
                P("samp"),
                P(None, "samp"),
                P(),
                P(None, "samp"),
                P(None, "samp"),
                P(None, "samp"),
            ),
            out_specs=(P(None, "samp"), P(None, "samp"), P(None, "samp"), P(None, "var")),
            check_vma=False,
        )(geno, *rest)

    return whole
```

```python
import functools

import jax
import jax.numpy as jnp
from jax import lax
from jax.experimental import pallas as pl
from jax.experimental.pallas import tpu as pltpu
from jax.sharding import PartitionSpec as P

MESH = pl.DeviceIdType.MESH
F32 = jnp.float32
BF16 = jnp.bfloat16


def log2(n):
    return n.bit_length() - 1


def split3(value):
    high = value.astype(BF16)
    rest = value - high.astype(F32)
    mid = rest.astype(BF16)
    low = (rest - mid.astype(F32)).astype(BF16)
    return high, mid, low


def sum3(value):
    rows = value.shape[0] // 3
    return value[:rows] + value[rows : 2 * rows] + value[2 * rows :]


def kernel(
    dims,
    geno_hbm, tgeno_hbm, pct_hbm, tpct_hbm, expo_hbm, perm_hbm, vc_hbm, sol_hbm, res_hbm, dir_hbm,
    osol_ref, ores_ref, odir_ref, oassoc_ref,
    vc_ref, perm_ref, pct_ref, tpct_ref, sol_ref, res_ref, dir_ref,
    graw, traw, gbf, tbf, table, tparts, row_of, lane_of, shuf, parts, lefts, squares, pacc, acc, image_ref, apart, bpart,
    psend, precv, pall, asend, arecv, az, aall, irecv, isend, fsend, frecv, fall, sums_z,
    isem, gsem, tsem, sem_ez, sem_ej, sem_sh, sem_p, sem_pa, sem_a, sem_az, sem_aa, sem_im, sem_f, sem_fa, sem_sz,
):
    NZ, NJ, NX, scale_rows = dims
    NY, NS = NJ // 2, NZ * NJ
    samp = lax.axis_index("samp")
    x = lax.axis_index("var")
    z = samp // NJ
    j = samp % NJ
    core = j % 2
    pair = j - core
    y = j // 2
    SP = dir_ref.shape[1]
    V = pct_ref.shape[1]
    TV = tpct_ref.shape[1]
    RP = SP // 128
    VB, VZ = V // NJ, V // NZ
    SQ = SP // NX
    W = min(SQ, 256)
    CW = SQ // W
    quarters = TV // 128
    chunks = graw.shape[0]
    crows = graw.shape[1]
    tchunks = traw.shape[0]
    trows = traw.shape[1]

    def loop(count, body):
        def step(i, carry):
            body(i)
            return carry

        lax.fori_loop(0, count, step, 0)

    def block(i, size):
        return pl.ds(pl.multiple_of(i * size, size), size)

    reads = [
        pltpu.make_async_copy(src, dst, isem.at[i])
        for i, (src, dst) in enumerate((
            (expo_hbm, table.at[core]), (pct_hbm, pct_ref), (perm_hbm, perm_ref), (dir_hbm, dir_ref),
            (res_hbm, res_ref), (tpct_hbm, tpct_ref), (sol_hbm, sol_ref), (vc_hbm, vc_ref),
        ))
    ]

    def gread(i):
        return pltpu.make_async_copy(geno_hbm.at[pl.ds(i * crows, crows), :], graw.at[i], gsem.at[i])

    def tread(i):
        return pltpu.make_async_copy(tgeno_hbm.at[pl.ds(i * trows, trows), :], traw.at[i], tsem.at[i])

    def outward(t, count):
        return (count // 2 + ((t + 1) // 2) * (2 * (t % 2) - 1)) % count

    def to_near(peer):
        return {"samp": z * NJ + peer}

    def nth_near(t):
        side = (core + t % 2 + t // (NJ - 2)) % 2
        return (pair + 2 * outward(t // 2, NY)) % NJ + side

    def to_z(peer):
        return {"samp": peer * NJ + j}

    def nth_z(t):
        return (z + outward(t, NZ)) % NZ

    def to_x(peer):
        return {"var": peer}

    def nth_x(t):
        return (x + outward(t, NX)) % NX

    def to_any(peer):
        return {"samp": peer}

    def nth_any(t):
        return (samp + NS // 2) % NS

    def device(dz, dy, side):
        return (z + dz) % NZ * NJ + (y + dy) % NY * 2 + side

    near = (NJ, nth_near, to_near)
    over_z = (NZ, nth_z, to_z)
    over_x = (NX, nth_x, to_x)
    everyone = (NS, nth_any, to_any)

    def each_peer(group, body, rolled=False):
        count, nth, _ = group
        if group is not everyone:
            if rolled:
                loop(count - 1, lambda t: body(nth(t)))
            else:
                for t in range(count - 1):
                    body(nth(t))
            return

        loop(NZ, lambda t: each_in_plane(t, body))

    def each_in_plane(t, body):
        first = (z + outward(t, NZ)) % NZ * NJ
        for k in range(NY):
            chip = first + (pair + 2 * outward(k, NY)) % NJ
            body(chip + 1 - core)
            if k < NY - 1:
                body(chip + core)
            else:
                pl.when(t < NZ - 1)(lambda chip=chip: body(chip + core))

    def push(group, src, dst, sem, peer, arrival=1):
        pltpu.make_async_remote_copy(
            src_ref=src, dst_ref=dst, send_sem=sem.at[0], recv_sem=sem.at[arrival],
            device_id=group[2](peer), device_id_type=MESH,
        ).start()

    def described(group, like, sem, arrival):
        return pltpu.make_async_remote_copy(
            src_ref=like, dst_ref=like, send_sem=sem.at[0], recv_sem=sem.at[arrival],
            device_id=group[2](group[1](0)), device_id_type=MESH,
        )

    def arrived(group, like, sem, arrival=1):
        described(group, like, sem, arrival).wait_recv()

    def sent(group, like, sem):
        described(group, like, sem, 1).wait_send()

    barrier = pltpu.get_barrier_semaphore()
    reads[0].start()
    for group in (near, over_z, over_x):
        each_peer(
            group,
            lambda peer, group=group: pl.semaphore_signal(
                barrier, inc=1, device_id=group[2](peer), device_id_type=MESH
            ),
        )
    for side in range(2):
        pl.semaphore_signal(barrier, inc=1, device_id=to_any(device(1, 1, side)), device_id_type=MESH)
    for copy in reads[1:]:
        copy.start()
    loop(chunks, lambda i: gread(i).start())
    loop(tchunks, lambda i: tread(i).start())
    pl.semaphore_wait(barrier, NJ + NZ + NX - 1)

    layers = 2 * NY + 3 * core
    each_peer(
        over_z, lambda peer: push(over_z, expo_hbm, table.at[layers + (z - peer + NZ) % NZ - 1], sem_ez, peer)
    )
    for dy in (2, 1, 3, 0):
        for side in (1 - core, core)[: 1 if dy == 0 else 2]:
            push(everyone, expo_hbm, table.at[2 * dy + core], sem_ej, device(0, NY - dy, side), 3 if dy == 2 else 1)
    for side in range(2):
        push(everyone, expo_hbm, table.at[14 + core], sem_ej, device(NZ - 1, NY - 1, side))

    reads[1].wait()
    reads[5].wait()
    pct = pct_ref[...].astype(F32)
    tpct = tpct_ref[...].astype(F32)

    def convert(i):
        gread(i).wait()

        def rows(r):
            codes = graw[i, block(r, 32), :].astype(F32)
            gbf[block(i * (crows // 32) + r, 32), :] = (codes * 50.0 - pct).astype(BF16)

        loop(crows // 32, rows)

    def tconvert(i):
        tread(i).wait()

        def rows(r):
            codes = traw[i, block(r, 64), :].astype(F32)
            tbf[block(i * (trows // 64) + r, 64), :] = (codes * 50.0 - tpct).astype(BF16)

        loop(trows // 64, rows)

    loop(chunks // 2, convert)

    reads[0].wait()
    arrived(over_z, table.at[pl.ds(0, NZ - 1)], sem_ez)

    push(near, table.at[pl.ds(layers, 3)], table.at[pl.ds(layers, 3)], sem_ej, pair + 1 - core)
    for dy, skip, start in ((3, 0, 26), (1, 1, 16)):
        size = 3 - skip
        for side in range(2):
            push(
                everyone, table.at[pl.ds(layers + skip, size)], table.at[pl.ds(start + size * core, size)],
                sem_ej, device(0, NY - dy, side), 2,
            )
    arrived(near, table.at[pl.ds(0, 2)], sem_ej, 3)
    each_peer(
        over_z,
        lambda peer: push(
            over_z, table.at[pl.ds(4, 2)], table.at[pl.ds(18 + 2 * ((z - peer + NZ) % NZ), 2)], sem_ej, peer, 2
        ),
    )

    loop(chunks - chunks // 2, lambda i: convert(chunks // 2 + i))
    freq = pct / 100.0
    square = 1.0 / (2.0 * freq * (1.0 - freq)) / 2500.0
    for i in range(V // 128):
        squares[i] = square[:, i * 128 : (i + 1) * 128]
    for i in (2, 3, 4, 6, 7):
        reads[i].wait()

    rows_half = NS * RP // 2
    index = perm_ref[:, block(x, SQ)]
    dz = ((index >> log2(SP * NJ)) - z) & (NZ - 1)
    dy = ((index >> log2(2 * SP)) - y) & (NY - 1)
    side = (index >> log2(SP)) & 1
    early = jnp.where(dz == 0, 2 * dy + side, jnp.where(dy == 0, 7 + 3 * side + dz, 14 + side))
    late = jnp.where(dy == 1, 14 + 2 * side + dz, jnp.where(dy == 2, 18 + 2 * dz + side, 25 + 3 * side + dz))
    place = jnp.where((dz == 0) | (dy == 0) | ((dz == 1) & (dy == 1)), early, late)
    row = place * RP + ((index >> 7) & (RP - 1))
    for b in range(8):
        row_of[b] = row[b : b + 1]
        lane_of[b] = index[b : b + 1] & 127
    sublane = lax.broadcasted_iota(jnp.int32, (8, W), 0)
    deep = lax.broadcasted_iota(jnp.int32, (rows_half, W), 0)
    lanes = lax.broadcasted_iota(jnp.int32, (128, W), 0)
    for h in range(2):
        arrived(near, table.at[pl.ds(0, 10 + 6 * h)], sem_ej, 1 + h)
        flat = table[16 * h : 16 * h + 16].reshape(rows_half, 128)
        for k, part in enumerate(split3(flat.T)):
            tparts[128 * k : 128 * k + 128, :] = part

        def lookup(c, h=h):
            cols = block(c, W)

            found = jnp.zeros((8, W), F32)
            for b in range(8):
                onehot = jnp.where(deep == row_of[b, :, cols] - h * rows_half, 1.0, 0.0).astype(BF16)
                picked = sum3(jnp.dot(tparts[...], onehot, preferred_element_type=F32))
                value = jnp.sum(jnp.where(lanes == lane_of[b, :, cols], picked, 0.0), axis=0, keepdims=True)
                found = jnp.where(sublane == b, value, found)
            mine = x * CW + c
            if h == 0:
                shuf[mine] = found
            else:
                shuf[mine] = shuf[mine] + found
                each_peer(over_x, lambda peer: push(over_x, shuf.at[mine], shuf.at[mine], sem_sh, peer))

        loop(CW, lookup)


    def stack(value, i):
        for k, part in enumerate(split3(jnp.concatenate([value, shuf[i] * value], axis=0))):
            parts[16 * k : 16 * k + 16, block(i, W)] = part

    def stack_dir(i):
        stack(dir_ref[:, block(i, W)], i)

    def on_part(q, t):
        return jnp.dot(parts[:, block(q, SQ)], gbf[block(q, SQ), block(t, VB)], preferred_element_type=F32)

    loop(CW, lambda i: stack_dir(x * CW + i))

    def own_products(i):
        for t in (2 * i, 2 * i + 1):
            pacc[t] = on_part(x, t)

    loop(NJ // 2, own_products)
    loop(tchunks, tconvert)
    arrived(over_x, shuf.at[pl.ds(0, CW * (NX - 1))], sem_sh)
    loop(CW * (NX - 1), lambda i: stack_dir((x * CW + CW + i) % (NX * CW)))

    def product(layer, half):
        t = layer * (VZ // VB) + half
        total = pacc[t]
        for k in range(1, NX):
            total = total + on_part((x + k) % NX, t)
        total = sum3(total)
        for k in range(VB // 128):
            for h in range(2):
                owner = layer * NJ + 2 * (half * (VB // 128) + k) + h
                psend[owner] = total[8 * h : 8 * h + 8, 128 * k : 128 * k + 128]

    def layer_step(t):
        for half in range(VZ // VB):
            product((z + outward(t, NZ)) % NZ, half)
        each_in_plane(t, lambda peer: push(everyone, psend.at[peer], precv.at[samp], sem_p, peer))

    loop(NZ, layer_step)
    precv[samp] = psend[samp]

    loop(SP // W, lambda i: stack(res_ref[:, block(i, W)], i))
    TW = min(TV, 256)

    def ascore(i):
        cols = block(i, TW)
        apart[:, cols] = sum3(jnp.dot(parts[...], tbf[:, cols], preferred_element_type=F32))

    loop(TV // TW, ascore)
    spots = []
    for i in range(NJ):
        h, q = divmod(i, quarters)
        spots.append((slice(8 * h, 8 * h + 8), slice(128 * q, 128 * q + 128)))
    for i, spot in enumerate(spots):
        asend[i] = apart[spot]
    each_peer(near, lambda peer: push(near, asend.at[peer], arecv.at[j], sem_a, peer))
    arecv[j] = asend[j]

    arrived(everyone, precv.at[pl.ds(0, NS - 1)], sem_p)
    total = precv[0]
    for i in range(1, NS):
        total = total + precv[i]
    pall[samp] = total

    def share_sums(t):
        each_in_plane(t, lambda peer: push(everyone, pall.at[samp], pall.at[samp], sem_pa, peer, 2 - t // (NZ - 1)))

    loop(NZ, share_sums)

    arrived(near, arecv.at[pl.ds(0, NJ - 1)], sem_a)
    total = arecv[0]
    for i in range(1, NJ):
        total = total + arecv[i]
    az[z] = total
    each_peer(over_z, lambda peer: push(over_z, az.at[z], az.at[z], sem_az, peer))
    def scaled(layer, place):
        for k in range(NY):
            chip = layer * NY + k
            sums = jnp.concatenate([pall[2 * chip], pall[2 * chip + 1]], axis=0) * squares[chip]
            for i, part in enumerate(split3(sums)):
                lefts[place, 16 * i : 16 * i + 16, k * 128 : (k + 1) * 128] = part

    def against(place, rows):
        return lax.dot_general(
            lefts[place], gbf[rows, block((z + place) % NZ, VZ)], (((1,), (1,)), ((), ())), preferred_element_type=F32
        )

    arrived(everyone, pall.at[pl.ds(0, NJ - 1)], sem_pa, 1)
    scaled(z, 0)

    def own_parts(i):
        for q in (2 * i, 2 * i + 1):
            acc[q] = against(0, block(q, SQ))

    loop(NX // 2, own_parts)
    arrived(everyone, pall.at[pl.ds(0, NS - NJ)], sem_pa, 2)
    loop(NZ - 1, lambda k: scaled((z + k + 1) % NZ, k + 1))

    def part(q):
        total = acc[q]
        for k in range(1, NZ):
            total = total + against(k, block(q, SQ))
        value = sum3(total)
        for c in range(CW):
            cols = slice(c * W, (c + 1) * W)
            isend[q, :, cols] = (
                vc_ref[1] * value[0:8, cols] + vc_ref[2] * shuf[q * CW + c] * value[8:16, cols]
            ) * (1.0 / scale_rows)
        each_peer(over_x, lambda peer: push(over_x, isend.at[q], irecv.at[q, x], sem_im.at[q], peer))
        irecv[q, x] = isend[q]

    loop(NX, part)

    arrived(over_z, az.at[pl.ds(0, NZ - 1)], sem_az)
    total = az[0]
    for i in range(1, NZ):
        total = total + az[i]
    aall[j] = total
    each_peer(near, lambda peer: push(near, aall.at[j], aall.at[j], sem_aa, peer))
    sent(over_z, table.at[pl.ds(0, NZ - 1)], sem_ez)
    sent(near, table.at[pl.ds(0, 28)], sem_ej)
    sent(over_x, shuf.at[pl.ds(0, CW * (NX - 1))], sem_sh)
    sent(everyone, psend.at[pl.ds(0, NS - 1)], sem_p)
    sent(everyone, pall.at[pl.ds(0, NS - 1)], sem_pa)
    sent(near, asend.at[pl.ds(0, NJ - 1)], sem_a)
    bpart[...] = jnp.zeros_like(bpart)

    def score(q, sums):
        arrived(over_x, irecv.at[q, pl.ds(0, NX - 1)], sem_im.at[q])
        image = irecv[q, 0]
        for i in range(1, NX):
            image = image + irecv[q, i]
        cols = block(q, SQ)
        d, r = dir_ref[:, cols], res_ref[:, cols]
        image = vc_ref[0] * d + image
        image_ref[:, cols] = image
        for c in range(CW):
            stack(image[:, c * W : (c + 1) * W], q * CW + c)
        bpart[...] += sum3(jnp.dot(parts[:, cols], tbf[cols, :], preferred_element_type=F32))
        sums = list(sums)
        for k, term in enumerate((r * r, d * image, r * image, image * image)):
            for c in range(SQ // 128):
                sums[k] = sums[k] + term[:, 128 * c : 128 * c + 128]
        return tuple(sums)

    sums = lax.fori_loop(0, NX, score, (jnp.zeros((8, 128), F32),) * 4)
    lane = lax.broadcasted_iota(jnp.int32, (8, 128), 1) - lax.broadcasted_iota(jnp.int32, (8, 128), 0)
    scalars = jnp.zeros((8, 128), F32)
    for k in range(4):
        scalars = jnp.where(lane == 8 * k, jnp.sum(sums[k], axis=1, keepdims=True), scalars)
    scalars = jnp.broadcast_to(jnp.sum(scalars, axis=0, keepdims=True), (8, 128))
    for i, spot in enumerate(spots):
        fsend[i, 0] = bpart[spot]
        fsend[i, 1] = scalars
    each_peer(near, lambda peer: push(near, fsend.at[peer], frecv.at[j], sem_f, peer))
    frecv[j] = fsend[j]
    for q in range(NX):
        sent(over_x, isend.at[pl.ds(0, NX - 1)], sem_im.at[q])
    arrived(near, frecv.at[pl.ds(0, NJ - 1)], sem_f)
    total = frecv[0]
    for i in range(1, NJ):
        total = total + frecv[i]
    fall[samp] = total[0]
    sums_z[z] = total[1]
    each_peer(everyone, lambda peer: push(everyone, fall.at[samp], fall.at[samp], sem_fa, peer))
    each_peer(over_z, lambda peer: push(over_z, sums_z.at[z], sums_z.at[z], sem_sz, peer))
    arrived(over_z, sums_z.at[pl.ds(0, NZ - 1)], sem_sz)
    row = sums_z[0]
    for i in range(1, NZ):
        row = row + sums_z[i]
    norm_now, curvature, cross, square = (
        jnp.sum(jnp.where(lane == 8 * k, row, 0.0), axis=1, keepdims=True) for k in range(4)
    )
    alpha = norm_now / curvature

    norm_next = norm_now - 2.0 * alpha * cross + alpha * alpha * square
    beta = norm_next / norm_now
    d = dir_ref[...]
    new_res = res_ref[...] - alpha * image_ref[...]
    osol_ref[...] = sol_ref[...] + alpha * d
    ores_ref[...] = new_res
    odir_ref[...] = new_res + beta * d
    sent(near, fsend.at[pl.ds(0, NJ - 1)], sem_f)
    sent(over_z, sums_z.at[pl.ds(0, NZ - 1)], sem_sz)

    tfreq = tpct / 100.0
    root = float(NS * SP) ** 0.5 * 50.0
    tscale = lax.rsqrt(2.0 * tfreq * (1.0 - tfreq)) / root
    arrived(everyone, fall.at[pl.ds(0, NS - 1)], sem_fa)
    sent(over_z, az.at[pl.ds(0, NZ - 1)], sem_az)
    sent(near, aall.at[pl.ds(0, NJ - 1)], sem_aa)
    arrived(near, aall.at[pl.ds(0, NJ - 1)], sem_aa)
    for i, spot in enumerate(spots):
        total = fall[i]
        for k in range(1, NZ):
            total = total + fall[k * NJ + i]
        oassoc_ref[spot] = (aall[i] - alpha * total) * tscale[:, spot[1]]
    sent(everyone, fall.at[pl.ds(0, NS - 1)], sem_fa)


def local(dims, geno, allele_pct, test_geno, test_pct, exposure, perm, var_comp, solution, resid, direction):
    NZ, NJ, NX, _ = dims
    SP, V = geno.shape
    TV = test_geno.shape[1]
    RP, VB, SQ = SP // 128, V // NJ, SP // NX
    W = min(SQ, 256)
    chunks, tchunks = 4, 1
    NS = NZ * NJ
    vmem = pl.BlockSpec(memory_space=pltpu.VMEM)
    hbm = pl.BlockSpec(memory_space=pltpu.HBM)
    dma = pltpu.SemaphoreType.DMA
    rhs = jax.ShapeDtypeStruct((8, SP), F32)
    outs = (rhs, rhs, rhs, jax.ShapeDtypeStruct((16, TV), F32))
    results = pl.pallas_call(
        functools.partial(kernel, dims),
        out_shape=outs,
        in_specs=[hbm] * 10,
        out_specs=(vmem, vmem, vmem, vmem),
        scratch_shapes=[
            pltpu.SMEM((3,), F32),
            pltpu.VMEM((8, SP), jnp.int32),
            pltpu.VMEM((1, V), jnp.int32),
            pltpu.VMEM((1, TV), jnp.int32),
            pltpu.VMEM((8, SP), F32),
            pltpu.VMEM((8, SP), F32),
            pltpu.VMEM((8, SP), F32),
            pltpu.VMEM((chunks, SP // chunks, V), jnp.int32),
            pltpu.VMEM((tchunks, SP // tchunks, TV), jnp.int32),
            pltpu.VMEM((SP, V), BF16),
            pltpu.VMEM((SP, TV), BF16),
            pltpu.VMEM((NS, RP, 128), F32),
            pltpu.VMEM((384, NS * RP // 2), BF16),
            pltpu.VMEM((8, 1, SQ), jnp.int32),
            pltpu.VMEM((8, 1, SQ), jnp.int32),
            pltpu.VMEM((SP // W, 8, W), F32),
            pltpu.VMEM((48, SP), BF16),
            pltpu.VMEM((NZ, 48, V // NZ), BF16),
            pltpu.VMEM((V // 128, 1, 128), F32),
            pltpu.VMEM((NJ, 48, VB), F32),
            pltpu.VMEM((NX, 48, SQ), F32),
            pltpu.VMEM((8, SP), F32),
            pltpu.VMEM((16, TV), F32),
            pltpu.VMEM((16, TV), F32),
            pltpu.VMEM((NS, 8, 128), F32),
            pltpu.VMEM((NS, 8, 128), F32),
            pltpu.VMEM((NS, 8, 128), F32),
            pltpu.VMEM((NJ, 8, 128), F32),
            pltpu.VMEM((NJ, 8, 128), F32),
            pltpu.VMEM((NZ, 8, 128), F32),
            pltpu.VMEM((NJ, 8, 128), F32),
            pltpu.VMEM((NX, NX, 8, SQ), F32),
            pltpu.VMEM((NX, 8, SQ), F32),
            pltpu.VMEM((NJ, 2, 8, 128), F32),
            pltpu.VMEM((NJ, 2, 8, 128), F32),
            pltpu.VMEM((NS, 8, 128), F32),
            pltpu.VMEM((NZ, 8, 128), F32),
            dma((8,)),
            dma((chunks,)),
            dma((tchunks,)),
            dma((2,)),
            dma((4,)),
            dma((2,)),
            dma((2,)),
            dma((3,)),
            dma((2,)),
            dma((2,)),
            dma((2,)),
            dma((NX, 2)),
            dma((2,)),
            dma((2,)),
            dma((2,)),
        ],
        compiler_params=pltpu.CompilerParams(
            collective_id=0, has_side_effects=True, vmem_limit_bytes=40 * 1024 * 1024
        ),
    )(
        *(
            pltpu.with_memory_space_constraint(value, pltpu.HBM)
            for value in (
                geno,
                test_geno,
                allele_pct.reshape(1, V),
                test_pct.reshape(1, TV),
                exposure.reshape(RP, 128),
                perm,
                var_comp,
                solution,
                resid,
                direction,
            )
        )
    )
    return pl.pallas_call(
        hand_over,
        out_shape=outs,
        in_specs=[vmem] * 4,
        out_specs=(vmem,) * 4,
        compiler_params=pltpu.CompilerParams(vmem_limit_bytes=2 * 1024 * 1024),
    )(*results)


def hand_over(*refs):
    for source, target in zip(refs[:4], refs[4:]):
        target[...] = source[...]


def solution(mesh):
    samp, var = mesh.shape["samp"], mesh.shape["var"]
    near = 8 if samp == 32 else samp // 2

    def whole(geno, *rest):
        dims = (samp // near, near, var, float(geno.shape[1]))
        return jax.shard_map(
            functools.partial(local, dims),
            mesh=mesh,
            in_specs=(
                P("samp", "var"),
                P("var"),
                P("samp", "var"),
                P("var"),
                P("samp"),
                P(None, "samp"),
                P(),
                P(None, "samp"),
                P(None, "samp"),
                P(None, "samp"),
            ),
            out_specs=(P(None, "samp"), P(None, "samp"), P(None, "samp"), P(None, "var")),
            check_vma=False,
        )(geno, *rest)

    return whole
```

```python
import functools

import jax
import jax.numpy as jnp
from jax import lax
from jax.experimental import pallas as pl
from jax.experimental.pallas import tpu as pltpu
from jax.sharding import PartitionSpec as P

MESH = pl.DeviceIdType.MESH
F32 = jnp.float32
BF16 = jnp.bfloat16


def log2(n):
    return n.bit_length() - 1


def split3(value):
    high = value.astype(BF16)
    rest = value - high.astype(F32)
    mid = rest.astype(BF16)
    low = (rest - mid.astype(F32)).astype(BF16)
    return high, mid, low


def sum3(value):
    rows = value.shape[0] // 3
    return value[:rows] + value[rows : 2 * rows] + value[2 * rows :]


def kernel(
    dims,
    geno_hbm, tgeno_hbm, pct_hbm, tpct_hbm, expo_hbm, perm_hbm, vc_hbm, sol_hbm, res_hbm, dir_hbm,
    osol_ref, ores_ref, odir_ref, oassoc_ref,
    vc_ref, perm_ref, pct_ref, tpct_ref, sol_ref, res_ref, dir_ref,
    graw, traw, gbf, tbf, table, tparts, row_of, lane_of, shuf, parts, lefts, squares, pacc, acc, image_ref, apart, bpart,
    psend, precv, pall, asend, arecv, az, aall, irecv, isend, fsend, frecv, fall, srecv, sums_z,
    isem, gsem, tsem, sem_ez, sem_ej, sem_sh, sem_p, sem_pa, sem_a, sem_az, sem_aa, sem_im, sem_f, sem_fa, sem_s, sem_sz,
):
    NZ, NJ, NX, scale_rows = dims
    NY, NS = NJ // 2, NZ * NJ
    samp = lax.axis_index("samp")
    x = lax.axis_index("var")
    z = samp // NJ
    j = samp % NJ
    core = j % 2
    pair = j - core
    y = j // 2
    SP = dir_ref.shape[1]
    V = pct_ref.shape[1]
    TV = tpct_ref.shape[1]
    RP = SP // 128
    VB, VZ = V // NJ, V // NZ
    SQ = SP // NX
    W = min(SQ, 256)
    CW = SQ // W
    quarters = TV // 128
    chunks = graw.shape[0]
    crows = graw.shape[1]
    tchunks = traw.shape[0]
    trows = traw.shape[1]

    def loop(count, body):
        def step(i, carry):
            body(i)
            return carry

        lax.fori_loop(0, count, step, 0)

    def block(i, size):
        return pl.ds(pl.multiple_of(i * size, size), size)

    reads = [
        pltpu.make_async_copy(src, dst, isem.at[i])
        for i, (src, dst) in enumerate((
            (expo_hbm, table.at[core]), (pct_hbm, pct_ref), (perm_hbm, perm_ref), (dir_hbm, dir_ref),
            (res_hbm, res_ref), (tpct_hbm, tpct_ref), (sol_hbm, sol_ref), (vc_hbm, vc_ref),
        ))
    ]

    def gread(i):
        return pltpu.make_async_copy(geno_hbm.at[pl.ds(i * crows, crows), :], graw.at[i], gsem.at[i])

    def tread(i):
        return pltpu.make_async_copy(tgeno_hbm.at[pl.ds(i * trows, trows), :], traw.at[i], tsem.at[i])

    def outward(t, count):
        return (count // 2 + ((t + 1) // 2) * (2 * (t % 2) - 1)) % count

    def to_near(peer):
        return {"samp": z * NJ + peer}

    def nth_near(t):
        side = (core + t % 2 + t // (NJ - 2)) % 2
        return (pair + 2 * outward(t // 2, NY)) % NJ + side

    def to_z(peer):
        return {"samp": peer * NJ + j}

    def nth_z(t):
        return (z + outward(t, NZ)) % NZ

    def to_x(peer):
        return {"var": peer}

    def nth_x(t):
        return (x + outward(t, NX)) % NX

    def to_any(peer):
        return {"samp": peer}

    def nth_any(t):
        return (samp + NS // 2) % NS

    def device(dz, dy, side):
        return (z + dz) % NZ * NJ + (y + dy) % NY * 2 + side

    near = (NJ, nth_near, to_near)
    over_z = (NZ, nth_z, to_z)
    over_x = (NX, nth_x, to_x)
    everyone = (NS, nth_any, to_any)

    def each_peer(group, body, rolled=False):
        count, nth, _ = group
        if group is not everyone:
            if rolled:
                loop(count - 1, lambda t: body(nth(t)))
            else:
                for t in range(count - 1):
                    body(nth(t))
            return

        loop(NZ, lambda t: each_in_plane(t, body))

    def each_in_plane(t, body):
        first = (z + outward(t, NZ)) % NZ * NJ
        for k in range(NY):
            chip = first + (pair + 2 * outward(k, NY)) % NJ
            body(chip + 1 - core)
            if k < NY - 1:
                body(chip + core)
            else:
                pl.when(t < NZ - 1)(lambda chip=chip: body(chip + core))

    def push(group, src, dst, sem, peer, arrival=1):
        pltpu.make_async_remote_copy(
            src_ref=src, dst_ref=dst, send_sem=sem.at[0], recv_sem=sem.at[arrival],
            device_id=group[2](peer), device_id_type=MESH,
        ).start()

    def described(group, like, sem, arrival):
        return pltpu.make_async_remote_copy(
            src_ref=like, dst_ref=like, send_sem=sem.at[0], recv_sem=sem.at[arrival],
            device_id=group[2](group[1](0)), device_id_type=MESH,
        )

    def arrived(group, like, sem, arrival=1):
        described(group, like, sem, arrival).wait_recv()

    def sent(group, like, sem):
        described(group, like, sem, 1).wait_send()

    barrier = pltpu.get_barrier_semaphore()
    reads[0].start()
    for group in (near, over_z, over_x):
        each_peer(
            group,
            lambda peer, group=group: pl.semaphore_signal(
                barrier, inc=1, device_id=group[2](peer), device_id_type=MESH
            ),
        )
    for side in range(2):
        pl.semaphore_signal(barrier, inc=1, device_id=to_any(device(1, 1, side)), device_id_type=MESH)
    for copy in reads[1:]:
        copy.start()
    loop(chunks, lambda i: gread(i).start())
    loop(tchunks, lambda i: tread(i).start())
    pl.semaphore_wait(barrier, NJ + NZ + NX - 1)

    layers = 2 * NY + 3 * core
    reads[0].wait()
    mine = table.at[core]
    each_peer(
        over_z, lambda peer: push(over_z, mine, table.at[layers + (z - peer + NZ) % NZ - 1], sem_ez, peer)
    )
    for dy in (2, 1, 3, 0):
        for side in (1 - core, core)[: 1 if dy == 0 else 2]:
            push(everyone, mine, table.at[2 * dy + core], sem_ej, device(0, NY - dy, side), 3 if dy == 2 else 1)
    for side in range(2):
        push(everyone, mine, table.at[14 + core], sem_ej, device(NZ - 1, NY - 1, side))

    reads[1].wait()
    reads[5].wait()
    pct = pct_ref[...].astype(F32)
    tpct = tpct_ref[...].astype(F32)

    def convert(i):
        gread(i).wait()

        def rows(r):
            codes = graw[i, block(r, 32), :].astype(F32)
            gbf[block(i * (crows // 32) + r, 32), :] = (codes * 50.0 - pct).astype(BF16)

        loop(crows // 32, rows)

    def tconvert(i):
        tread(i).wait()

        def rows(r):
            codes = traw[i, block(r, 64), :].astype(F32)
            tbf[block(i * (trows // 64) + r, 64), :] = (codes * 50.0 - tpct).astype(BF16)

        loop(trows // 64, rows)

    loop(chunks // 2, convert)

    arrived(over_z, table.at[pl.ds(0, NZ - 1)], sem_ez)

    push(near, table.at[pl.ds(layers, 3)], table.at[pl.ds(layers, 3)], sem_ej, pair + 1 - core)
    for dy, skip, start in ((3, 0, 26), (1, 1, 16)):
        size = 3 - skip
        for side in range(2):
            push(
                everyone, table.at[pl.ds(layers + skip, size)], table.at[pl.ds(start + size * core, size)],
                sem_ej, device(0, NY - dy, side), 2,
            )
    arrived(near, table.at[pl.ds(0, 2)], sem_ej, 3)
    each_peer(
        over_z,
        lambda peer: push(
            over_z, table.at[pl.ds(4, 2)], table.at[pl.ds(18 + 2 * ((z - peer + NZ) % NZ), 2)], sem_ej, peer, 2
        ),
    )

    loop(chunks - chunks // 2, lambda i: convert(chunks // 2 + i))
    freq = pct / 100.0
    square = 1.0 / (2.0 * freq * (1.0 - freq)) / 2500.0
    for i in range(V // 128):
        squares[i] = square[:, i * 128 : (i + 1) * 128]
    for i in (2, 3, 4, 6, 7):
        reads[i].wait()

    rows_half = NS * RP // 2
    index = perm_ref[:, block(x, SQ)]
    dz = ((index >> log2(SP * NJ)) - z) & (NZ - 1)
    dy = ((index >> log2(2 * SP)) - y) & (NY - 1)
    side = (index >> log2(SP)) & 1
    early = jnp.where(dz == 0, 2 * dy + side, jnp.where(dy == 0, 7 + 3 * side + dz, 14 + side))
    late = jnp.where(dy == 1, 14 + 2 * side + dz, jnp.where(dy == 2, 18 + 2 * dz + side, 25 + 3 * side + dz))
    place = jnp.where((dz == 0) | (dy == 0) | ((dz == 1) & (dy == 1)), early, late)
    row = place * RP + ((index >> 7) & (RP - 1))
    for b in range(8):
        row_of[b] = row[b : b + 1]
        lane_of[b] = index[b : b + 1] & 127
    sublane = lax.broadcasted_iota(jnp.int32, (8, W), 0)
    deep = lax.broadcasted_iota(jnp.int32, (rows_half, W), 0)
    lanes = lax.broadcasted_iota(jnp.int32, (128, W), 0)
    for h in range(2):
        arrived(near, table.at[pl.ds(0, 10 + 6 * h)], sem_ej, 1 + h)
        flat = table[16 * h : 16 * h + 16].reshape(rows_half, 128)
        for k, part in enumerate(split3(flat.T)):
            tparts[128 * k : 128 * k + 128, :] = part

        def lookup(c, h=h):
            cols = block(c, W)

            found = jnp.zeros((8, W), F32)
            for b in range(8):
                onehot = jnp.where(deep == row_of[b, :, cols] - h * rows_half, 1.0, 0.0).astype(BF16)
                picked = sum3(jnp.dot(tparts[...], onehot, preferred_element_type=F32))
                value = jnp.sum(jnp.where(lanes == lane_of[b, :, cols], picked, 0.0), axis=0, keepdims=True)
                found = jnp.where(sublane == b, value, found)
            own = x * CW + c
            if h == 0:
                shuf[own] = found
            else:
                shuf[own] = shuf[own] + found
                each_peer(over_x, lambda peer: push(over_x, shuf.at[own], shuf.at[own], sem_sh, peer, (x - peer + NX) % NX))

        loop(CW, lookup)


    def stack(value, i):
        for k, part in enumerate(split3(jnp.concatenate([value, shuf[i] * value], axis=0))):
            parts[16 * k : 16 * k + 16, block(i, W)] = part

    def stack_dir(i):
        stack(dir_ref[:, block(i, W)], i)

    def on_part(q, t):
        return jnp.dot(parts[:, block(q, SQ)], gbf[block(q, SQ), block(t, VB)], preferred_element_type=F32)

    loop(CW, lambda i: stack_dir(x * CW + i))

    def own_products(i):
        for t in (2 * i, 2 * i + 1):
            pacc[t] = on_part(x, t)

    loop(NJ // 2, own_products)
    loop(tchunks, tconvert)
    for k in sorted(range(1, NX), key=lambda k: min(k, NX - k)):
        arrived(over_x, shuf.at[pl.ds(0, CW)], sem_sh, k)
        loop(CW, lambda i, k=k: stack_dir((x + k) % NX * CW + i))

    def product(layer, half):
        t = layer * (VZ // VB) + half
        total = pacc[t]
        for k in range(1, NX):
            total = total + on_part((x + k) % NX, t)
        total = sum3(total)
        for k in range(VB // 128):
            for h in range(2):
                owner = layer * NJ + 2 * (half * (VB // 128) + k) + h
                psend[owner] = total[8 * h : 8 * h + 8, 128 * k : 128 * k + 128]

    def layer_step(t):
        for half in range(VZ // VB):
            product((z + outward(t, NZ)) % NZ, half)
        each_in_plane(t, lambda peer: push(everyone, psend.at[peer], precv.at[samp], sem_p, peer))

    loop(NZ, layer_step)
    precv[samp] = psend[samp]

    loop(SP // W, lambda i: stack(res_ref[:, block(i, W)], i))
    TW = min(TV, 256)

    def ascore(i):
        cols = block(i, TW)
        apart[:, cols] = sum3(jnp.dot(parts[...], tbf[:, cols], preferred_element_type=F32))

    loop(TV // TW, ascore)
    spots = []
    for i in range(NJ):
        h, q = divmod(i, quarters)
        spots.append((slice(8 * h, 8 * h + 8), slice(128 * q, 128 * q + 128)))
    for i, spot in enumerate(spots):
        asend[i] = apart[spot]
    each_peer(near, lambda peer: push(near, asend.at[peer], arecv.at[j], sem_a, peer))
    arecv[j] = asend[j]

    arrived(everyone, precv.at[pl.ds(0, NS - 1)], sem_p)
    total = precv[0]
    for i in range(1, NS):
        total = total + precv[i]
    pall[samp] = total

    def share_sums(t):
        offset = (NZ - outward(t, NZ)) % NZ
        each_in_plane(t, lambda peer: push(everyone, pall.at[samp], pall.at[samp], sem_pa, peer, 1 + offset))

    loop(NZ, lambda i: share_sums(i * (NZ - 1) % NZ))

    arrived(near, arecv.at[pl.ds(0, NJ - 1)], sem_a)
    total = arecv[0]
    for i in range(1, NJ):
        total = total + arecv[i]
    az[z] = total
    each_peer(over_z, lambda peer: push(over_z, az.at[z], az.at[z], sem_az, peer))
    def scaled(layer, place):
        for k in range(NY):
            chip = layer * NY + k
            sums = jnp.concatenate([pall[2 * chip], pall[2 * chip + 1]], axis=0) * squares[chip]
            for i, part in enumerate(split3(sums)):
                lefts[place, 16 * i : 16 * i + 16, k * 128 : (k + 1) * 128] = part

    def against(place, rows):
        return lax.dot_general(
            lefts[place], gbf[rows, block((z + place) % NZ, VZ)], (((1,), (1,)), ((), ())), preferred_element_type=F32
        )

    arrived(everyone, pall.at[pl.ds(0, NJ - 1)], sem_pa, 1)
    scaled(z, 0)

    def own_parts(i):
        for q in (2 * i, 2 * i + 1):
            acc[q] = against(0, block(q, SQ))

    loop(NX // 2, own_parts)
    for k in sorted(range(1, NZ), key=lambda k: min(k, NZ - k)):
        arrived(everyone, pall.at[pl.ds(0, NJ)], sem_pa, 1 + k)
        scaled((z + k) % NZ, k)

    def part(q):
        total = acc[q]
        for k in range(1, NZ):
            total = total + against(k, block(q, SQ))
        value = sum3(total)
        for c in range(CW):
            cols = slice(c * W, (c + 1) * W)
            isend[q, :, cols] = (
                vc_ref[1] * value[0:8, cols] + vc_ref[2] * shuf[q * CW + c] * value[8:16, cols]
            ) * (1.0 / scale_rows)
        each_peer(over_x, lambda peer: push(over_x, isend.at[q], irecv.at[q, x], sem_im.at[q], peer))
        irecv[q, x] = isend[q]

    loop(NX, part)

    arrived(over_z, az.at[pl.ds(0, NZ - 1)], sem_az)
    total = az[0]
    for i in range(1, NZ):
        total = total + az[i]
    aall[j] = total
    each_peer(near, lambda peer: push(near, aall.at[j], aall.at[j], sem_aa, peer))
    sent(over_z, table.at[pl.ds(0, NZ - 1)], sem_ez)
    sent(near, table.at[pl.ds(0, 28)], sem_ej)
    sent(over_x, shuf.at[pl.ds(0, CW * (NX - 1))], sem_sh)
    sent(everyone, psend.at[pl.ds(0, NS - 1)], sem_p)
    sent(everyone, pall.at[pl.ds(0, NS - 1)], sem_pa)
    sent(near, asend.at[pl.ds(0, NJ - 1)], sem_a)
    bpart[...] = jnp.zeros_like(bpart)

    def score(q, sums):
        arrived(over_x, irecv.at[q, pl.ds(0, NX - 1)], sem_im.at[q])
        image = irecv[q, 0]
        for i in range(1, NX):
            image = image + irecv[q, i]
        cols = block(q, SQ)
        d, r = dir_ref[:, cols], res_ref[:, cols]
        image = vc_ref[0] * d + image
        image_ref[:, cols] = image
        for c in range(CW):
            stack(image[:, c * W : (c + 1) * W], q * CW + c)
        bpart[...] += sum3(jnp.dot(parts[:, cols], tbf[cols, :], preferred_element_type=F32))
        sums = list(sums)
        for k, term in enumerate((r * r, d * image, r * image, image * image)):
            for c in range(SQ // 128):
                sums[k] = sums[k] + term[:, 128 * c : 128 * c + 128]
        return tuple(sums)

    sums = lax.fori_loop(0, NX, score, (jnp.zeros((8, 128), F32),) * 4)
    lane = lax.broadcasted_iota(jnp.int32, (8, 128), 1) - lax.broadcasted_iota(jnp.int32, (8, 128), 0)
    scalars = jnp.zeros((8, 128), F32)
    for k in range(4):
        scalars = jnp.where(lane == 8 * k, jnp.sum(sums[k], axis=1, keepdims=True), scalars)
    scalars = jnp.broadcast_to(jnp.sum(scalars, axis=0, keepdims=True), (8, 128))
    for i, spot in enumerate(spots):
        fsend[i] = bpart[spot]
    srecv[j] = scalars
    each_peer(near, lambda peer: push(near, fsend.at[peer], frecv.at[j], sem_f, peer))
    frecv[j] = fsend[j]
    each_peer(near, lambda peer: push(near, srecv.at[j], srecv.at[j], sem_s, peer))
    for q in range(NX):
        sent(over_x, isend.at[pl.ds(0, NX - 1)], sem_im.at[q])
    arrived(near, frecv.at[pl.ds(0, NJ - 1)], sem_f)
    total = frecv[0]
    for i in range(1, NJ):
        total = total + frecv[i]
    fall[samp] = total
    each_peer(everyone, lambda peer: push(everyone, fall.at[samp], fall.at[samp], sem_fa, peer))
    arrived(near, srecv.at[pl.ds(0, NJ - 1)], sem_s)
    total = srecv[0]
    for i in range(1, NJ):
        total = total + srecv[i]
    sums_z[z] = total
    each_peer(over_z, lambda peer: push(over_z, sums_z.at[z], sums_z.at[z], sem_sz, peer))
    arrived(over_z, sums_z.at[pl.ds(0, NZ - 1)], sem_sz)
    row = sums_z[0]
    for i in range(1, NZ):
        row = row + sums_z[i]
    norm_now, curvature, cross, square = (
        jnp.sum(jnp.where(lane == 8 * k, row, 0.0), axis=1, keepdims=True) for k in range(4)
    )
    alpha = norm_now / curvature

    norm_next = norm_now - 2.0 * alpha * cross + alpha * alpha * square
    beta = norm_next / norm_now
    d = dir_ref[...]
    new_res = res_ref[...] - alpha * image_ref[...]
    osol_ref[...] = sol_ref[...] + alpha * d
    ores_ref[...] = new_res
    odir_ref[...] = new_res + beta * d
    sent(near, fsend.at[pl.ds(0, NJ - 1)], sem_f)
    sent(near, srecv.at[pl.ds(0, NJ - 1)], sem_s)
    sent(over_z, sums_z.at[pl.ds(0, NZ - 1)], sem_sz)

    tfreq = tpct / 100.0
    root = float(NS * SP) ** 0.5 * 50.0
    tscale = lax.rsqrt(2.0 * tfreq * (1.0 - tfreq)) / root
    arrived(everyone, fall.at[pl.ds(0, NS - 1)], sem_fa)
    sent(over_z, az.at[pl.ds(0, NZ - 1)], sem_az)
    sent(near, aall.at[pl.ds(0, NJ - 1)], sem_aa)
    arrived(near, aall.at[pl.ds(0, NJ - 1)], sem_aa)
    for i, spot in enumerate(spots):
        total = fall[i]
        for k in range(1, NZ):
            total = total + fall[k * NJ + i]
        oassoc_ref[spot] = (aall[i] - alpha * total) * tscale[:, spot[1]]
    sent(everyone, fall.at[pl.ds(0, NS - 1)], sem_fa)


def local(dims, geno, allele_pct, test_geno, test_pct, exposure, perm, var_comp, solution, resid, direction):
    NZ, NJ, NX, _ = dims
    SP, V = geno.shape
    TV = test_geno.shape[1]
    RP, VB, SQ = SP // 128, V // NJ, SP // NX
    W = min(SQ, 256)
    chunks, tchunks = 4, 1
    NS = NZ * NJ
    vmem = pl.BlockSpec(memory_space=pltpu.VMEM)
    hbm = pl.BlockSpec(memory_space=pltpu.HBM)
    dma = pltpu.SemaphoreType.DMA
    rhs = jax.ShapeDtypeStruct((8, SP), F32)
    outs = (rhs, rhs, rhs, jax.ShapeDtypeStruct((16, TV), F32))
    results = pl.pallas_call(
        functools.partial(kernel, dims),
        out_shape=outs,
        in_specs=[hbm] * 10,
        out_specs=(vmem, vmem, vmem, vmem),
        scratch_shapes=[
            pltpu.SMEM((3,), F32),
            pltpu.VMEM((8, SP), jnp.int32),
            pltpu.VMEM((1, V), jnp.int32),
            pltpu.VMEM((1, TV), jnp.int32),
            pltpu.VMEM((8, SP), F32),
            pltpu.VMEM((8, SP), F32),
            pltpu.VMEM((8, SP), F32),
            pltpu.VMEM((chunks, SP // chunks, V), jnp.int32),
            pltpu.VMEM((tchunks, SP // tchunks, TV), jnp.int32),
            pltpu.VMEM((SP, V), BF16),
            pltpu.VMEM((SP, TV), BF16),
            pltpu.VMEM((NS, RP, 128), F32),
            pltpu.VMEM((384, NS * RP // 2), BF16),
            pltpu.VMEM((8, 1, SQ), jnp.int32),
            pltpu.VMEM((8, 1, SQ), jnp.int32),
            pltpu.VMEM((SP // W, 8, W), F32),
            pltpu.VMEM((48, SP), BF16),
            pltpu.VMEM((NZ, 48, V // NZ), BF16),
            pltpu.VMEM((V // 128, 1, 128), F32),
            pltpu.VMEM((NJ, 48, VB), F32),
            pltpu.VMEM((NX, 48, SQ), F32),
            pltpu.VMEM((8, SP), F32),
            pltpu.VMEM((16, TV), F32),
            pltpu.VMEM((16, TV), F32),
            pltpu.VMEM((NS, 8, 128), F32),
            pltpu.VMEM((NS, 8, 128), F32),
            pltpu.VMEM((NS, 8, 128), F32),
            pltpu.VMEM((NJ, 8, 128), F32),
            pltpu.VMEM((NJ, 8, 128), F32),
            pltpu.VMEM((NZ, 8, 128), F32),
            pltpu.VMEM((NJ, 8, 128), F32),
            pltpu.VMEM((NX, NX, 8, SQ), F32),
            pltpu.VMEM((NX, 8, SQ), F32),
            pltpu.VMEM((NJ, 8, 128), F32),
            pltpu.VMEM((NJ, 8, 128), F32),
            pltpu.VMEM((NS, 8, 128), F32),
            pltpu.VMEM((NJ, 8, 128), F32),
            pltpu.VMEM((NZ, 8, 128), F32),
            dma((8,)),
            dma((chunks,)),
            dma((tchunks,)),
            dma((2,)),
            dma((4,)),
            dma((NX,)),
            dma((2,)),
            dma((1 + NZ,)),
            dma((2,)),
            dma((2,)),
            dma((2,)),
            dma((NX, 2)),
            dma((2,)),
            dma((2,)),
            dma((2,)),
            dma((2,)),
        ],
        compiler_params=pltpu.CompilerParams(
            collective_id=0, has_side_effects=True, vmem_limit_bytes=40 * 1024 * 1024
        ),
    )(
        *(
            pltpu.with_memory_space_constraint(value, pltpu.HBM)
            for value in (
                geno,
                test_geno,
                allele_pct.reshape(1, V),
                test_pct.reshape(1, TV),
                exposure.reshape(RP, 128),
                perm,
                var_comp,
                solution,
                resid,
                direction,
            )
        )
    )
    return pl.pallas_call(
        hand_over,
        out_shape=outs,
        in_specs=[vmem] * 4,
        out_specs=(vmem,) * 4,
        compiler_params=pltpu.CompilerParams(vmem_limit_bytes=2 * 1024 * 1024),
    )(*results)


def hand_over(*refs):
    for source, target in zip(refs[:4], refs[4:]):
        target[...] = source[...]


def solution(mesh):
    samp, var = mesh.shape["samp"], mesh.shape["var"]
    near = 8 if samp == 32 else samp // 2

    def whole(geno, *rest):
        dims = (samp // near, near, var, float(geno.shape[1]))
        return jax.shard_map(
            functools.partial(local, dims),
            mesh=mesh,
            in_specs=(
                P("samp", "var"),
                P("var"),
                P("samp", "var"),
                P("var"),
                P("samp"),
                P(None, "samp"),
                P(),
                P(None, "samp"),
                P(None, "samp"),
                P(None, "samp"),
            ),
            out_specs=(P(None, "samp"), P(None, "samp"), P(None, "samp"), P(None, "var")),
            check_vma=False,
        )(geno, *rest)

    return whole
```

```python
import functools

import jax
import jax.numpy as jnp
from jax import lax
from jax.experimental import pallas as pl
from jax.experimental.pallas import tpu as pltpu
from jax.sharding import PartitionSpec as P

MESH = pl.DeviceIdType.MESH
F32 = jnp.float32
BF16 = jnp.bfloat16


def log2(n):
    return n.bit_length() - 1


def split3(value):
    high = value.astype(BF16)
    rest = value - high.astype(F32)
    mid = rest.astype(BF16)
    low = (rest - mid.astype(F32)).astype(BF16)
    return high, mid, low


def sum3(value):
    rows = value.shape[0] // 3
    return value[:rows] + value[rows : 2 * rows] + value[2 * rows :]


def kernel(
    dims,
    geno_hbm, tgeno_hbm, pct_hbm, tpct_hbm, expo_hbm, perm_hbm, vc_hbm, sol_hbm, res_hbm, dir_hbm,
    osol_ref, ores_ref, odir_ref, oassoc_ref,
    vc_ref, perm_ref, pct_ref, tpct_ref, sol_ref, res_ref, dir_ref,
    graw, traw, gbf, tbf, table, tparts, row_of, lane_of, shuf, parts, lefts, squares, pacc, acc, image_ref, apart, bpart,
    psend, precv, pall, asend, arecv, az, aall, irecv, isend, fsend, frecv, fall, sums_z,
    isem, gsem, tsem, sem_ez, sem_ej, sem_sh, sem_p, sem_pa, sem_a, sem_az, sem_aa, sem_im, sem_f, sem_fa, sem_sz,
):
    NZ, NJ, NX, scale_rows = dims
    NY, NS = NJ // 2, NZ * NJ
    samp = lax.axis_index("samp")
    x = lax.axis_index("var")
    z = samp // NJ
    j = samp % NJ
    core = j % 2
    pair = j - core
    y = j // 2
    SP = dir_ref.shape[1]
    V = pct_ref.shape[1]
    TV = tpct_ref.shape[1]
    RP = SP // 128
    VB, VZ = V // NJ, V // NZ
    SQ = SP // NX
    W = min(SQ, 256)
    CW = SQ // W
    quarters = TV // 128
    chunks = graw.shape[0]
    crows = graw.shape[1]
    tchunks = traw.shape[0]
    trows = traw.shape[1]

    def loop(count, body):
        def step(i, carry):
            body(i)
            return carry

        lax.fori_loop(0, count, step, 0)

    def block(i, size):
        return pl.ds(pl.multiple_of(i * size, size), size)

    reads = [
        pltpu.make_async_copy(src, dst, isem.at[i])
        for i, (src, dst) in enumerate((
            (expo_hbm, table.at[core]), (pct_hbm, pct_ref), (perm_hbm, perm_ref), (dir_hbm, dir_ref),
            (res_hbm, res_ref), (tpct_hbm, tpct_ref), (sol_hbm, sol_ref), (vc_hbm, vc_ref),
        ))
    ]

    def gread(i):
        return pltpu.make_async_copy(geno_hbm.at[pl.ds(i * crows, crows), :], graw.at[i], gsem.at[i])

    def tread(i):
        return pltpu.make_async_copy(tgeno_hbm.at[pl.ds(i * trows, trows), :], traw.at[i], tsem.at[i])

    def outward(t, count):
        return (count // 2 + ((t + 1) // 2) * (2 * (t % 2) - 1)) % count

    def to_near(peer):
        return {"samp": z * NJ + peer}

    def nth_near(t):
        side = (core + t % 2 + t // (NJ - 2)) % 2
        return (pair + 2 * outward(t // 2, NY)) % NJ + side

    def to_z(peer):
        return {"samp": peer * NJ + j}

    def nth_z(t):
        return (z + outward(t, NZ)) % NZ

    def to_x(peer):
        return {"var": peer}

    def nth_x(t):
        return (x + outward(t, NX)) % NX

    def to_any(peer):
        return {"samp": peer}

    def nth_any(t):
        return (samp + NS // 2) % NS

    def device(dz, dy, side):
        return (z + dz) % NZ * NJ + (y + dy) % NY * 2 + side

    near = (NJ, nth_near, to_near)
    over_z = (NZ, nth_z, to_z)
    over_x = (NX, nth_x, to_x)
    everyone = (NS, nth_any, to_any)

    def each_peer(group, body, rolled=False):
        count, nth, _ = group
        if group is not everyone:
            if rolled:
                loop(count - 1, lambda t: body(nth(t)))
            else:
                for t in range(count - 1):
                    body(nth(t))
            return

        loop(NZ, lambda t: each_in_plane(t, body))

    def each_in_plane(t, body):
        first = (z + outward(t, NZ)) % NZ * NJ
        for k in range(NY):
            chip = first + (pair + 2 * outward(k, NY)) % NJ
            body(chip + 1 - core)
            if k < NY - 1:
                body(chip + core)
            else:
                pl.when(t < NZ - 1)(lambda chip=chip: body(chip + core))

    def push(group, src, dst, sem, peer, arrival=1):
        pltpu.make_async_remote_copy(
            src_ref=src, dst_ref=dst, send_sem=sem.at[0], recv_sem=sem.at[arrival],
            device_id=group[2](peer), device_id_type=MESH,
        ).start()

    def described(group, like, sem, arrival):
        return pltpu.make_async_remote_copy(
            src_ref=like, dst_ref=like, send_sem=sem.at[0], recv_sem=sem.at[arrival],
            device_id=group[2](group[1](0)), device_id_type=MESH,
        )

    def arrived(group, like, sem, arrival=1):
        described(group, like, sem, arrival).wait_recv()

    def sent(group, like, sem):
        described(group, like, sem, 1).wait_send()

    barrier = pltpu.get_barrier_semaphore()
    reads[0].start()
    for group in (near, over_z, over_x):
        each_peer(
            group,
            lambda peer, group=group: pl.semaphore_signal(
                barrier, inc=1, device_id=group[2](peer), device_id_type=MESH
            ),
        )
    for side in range(2):
        pl.semaphore_signal(barrier, inc=1, device_id=to_any(device(1, 1, side)), device_id_type=MESH)
    for copy in reads[1:]:
        copy.start()
    loop(chunks, lambda i: gread(i).start())
    loop(tchunks, lambda i: tread(i).start())
    pl.semaphore_wait(barrier, NJ + NZ + NX - 1)

    layers = 2 * NY + 3 * core
    reads[0].wait()
    mine = table.at[core]
    each_peer(
        over_z, lambda peer: push(over_z, mine, table.at[layers + (z - peer + NZ) % NZ - 1], sem_ez, peer)
    )
    for dy in (2, 1, 3, 0):
        for side in (1 - core, core)[: 1 if dy == 0 else 2]:
            push(everyone, mine, table.at[2 * dy + core], sem_ej, device(0, NY - dy, side), 3 if dy == 2 else 1)
    for side in range(2):
        push(everyone, mine, table.at[14 + core], sem_ej, device(NZ - 1, NY - 1, side))

    reads[1].wait()
    reads[5].wait()
    pct = pct_ref[...].astype(F32)
    tpct = tpct_ref[...].astype(F32)

    def convert(i):
        gread(i).wait()

        def rows(r):
            codes = graw[i, block(r, 32), :].astype(F32)
            gbf[block(i * (crows // 32) + r, 32), :] = (codes * 50.0 - pct).astype(BF16)

        loop(crows // 32, rows)

    def tconvert(i):
        tread(i).wait()

        def rows(r):
            codes = traw[i, block(r, 64), :].astype(F32)
            tbf[block(i * (trows // 64) + r, 64), :] = (codes * 50.0 - tpct).astype(BF16)

        loop(trows // 64, rows)

    loop(chunks // 2, convert)

    arrived(over_z, table.at[pl.ds(0, NZ - 1)], sem_ez)

    push(near, table.at[pl.ds(layers, 3)], table.at[pl.ds(layers, 3)], sem_ej, pair + 1 - core)
    for dy, skip, start in ((3, 0, 26), (1, 1, 16)):
        size = 3 - skip
        for side in range(2):
            push(
                everyone, table.at[pl.ds(layers + skip, size)], table.at[pl.ds(start + size * core, size)],
                sem_ej, device(0, NY - dy, side), 2,
            )
    arrived(near, table.at[pl.ds(0, 2)], sem_ej, 3)
    each_peer(
        over_z,
        lambda peer: push(
            over_z, table.at[pl.ds(4, 2)], table.at[pl.ds(18 + 2 * ((z - peer + NZ) % NZ), 2)], sem_ej, peer, 2
        ),
    )

    loop(chunks - chunks // 2, lambda i: convert(chunks // 2 + i))
    freq = pct / 100.0
    square = 1.0 / (2.0 * freq * (1.0 - freq)) / 2500.0
    for i in range(V // 128):
        squares[i] = square[:, i * 128 : (i + 1) * 128]
    for i in (2, 3, 4, 6, 7):
        reads[i].wait()

    rows_half = NS * RP // 2
    index = perm_ref[:, block(x, SQ)]
    dz = ((index >> log2(SP * NJ)) - z) & (NZ - 1)
    dy = ((index >> log2(2 * SP)) - y) & (NY - 1)
    side = (index >> log2(SP)) & 1
    early = jnp.where(dz == 0, 2 * dy + side, jnp.where(dy == 0, 7 + 3 * side + dz, 14 + side))
    late = jnp.where(dy == 1, 14 + 2 * side + dz, jnp.where(dy == 2, 18 + 2 * dz + side, 25 + 3 * side + dz))
    place = jnp.where((dz == 0) | (dy == 0) | ((dz == 1) & (dy == 1)), early, late)
    row = place * RP + ((index >> 7) & (RP - 1))
    for b in range(8):
        row_of[b] = row[b : b + 1]
        lane_of[b] = index[b : b + 1] & 127
    sublane = lax.broadcasted_iota(jnp.int32, (8, W), 0)
    deep = lax.broadcasted_iota(jnp.int32, (rows_half, W), 0)
    lanes = lax.broadcasted_iota(jnp.int32, (128, W), 0)
    for h in range(2):
        arrived(near, table.at[pl.ds(0, 10 + 6 * h)], sem_ej, 1 + h)
        flat = table[16 * h : 16 * h + 16].reshape(rows_half, 128)
        for k, part in enumerate(split3(flat.T)):
            tparts[128 * k : 128 * k + 128, :] = part

        def lookup(c, h=h):
            cols = block(c, W)

            found = jnp.zeros((8, W), F32)
            for b in range(8):
                onehot = jnp.where(deep == row_of[b, :, cols] - h * rows_half, 1.0, 0.0).astype(BF16)
                picked = sum3(jnp.dot(tparts[...], onehot, preferred_element_type=F32))
                value = jnp.sum(jnp.where(lanes == lane_of[b, :, cols], picked, 0.0), axis=0, keepdims=True)
                found = jnp.where(sublane == b, value, found)
            own = x * CW + c
            if h == 0:
                shuf[own] = found
            else:
                shuf[own] = shuf[own] + found
                each_peer(over_x, lambda peer: push(over_x, shuf.at[own], shuf.at[own], sem_sh, peer))

        loop(CW, lookup)


    def stack(value, i):
        for k, part in enumerate(split3(jnp.concatenate([value, shuf[i] * value], axis=0))):
            parts[16 * k : 16 * k + 16, block(i, W)] = part

    def stack_dir(i):
        stack(dir_ref[:, block(i, W)], i)

    def on_part(q, t):
        return jnp.dot(parts[:, block(q, SQ)], gbf[block(q, SQ), block(t, VB)], preferred_element_type=F32)

    loop(CW, lambda i: stack_dir(x * CW + i))

    def own_products(i):
        for t in (2 * i, 2 * i + 1):
            pacc[t] = on_part(x, t)

    loop(NJ // 2, own_products)
    loop(tchunks, tconvert)
    arrived(over_x, shuf.at[pl.ds(0, CW * (NX - 1))], sem_sh)
    loop(CW * (NX - 1), lambda i: stack_dir((x * CW + CW + i) % (NX * CW)))

    def product(layer, half):
        t = layer * (VZ // VB) + half
        total = pacc[t]
        for k in range(1, NX):
            total = total + on_part((x + k) % NX, t)
        total = sum3(total)
        for k in range(VB // 128):
            for h in range(2):
                owner = layer * NJ + 2 * (half * (VB // 128) + k) + h
                psend[owner] = total[8 * h : 8 * h + 8, 128 * k : 128 * k + 128]

    def layer_step(t):
        for half in range(VZ // VB):
            product((z + outward(t, NZ)) % NZ, half)
        each_in_plane(t, lambda peer: push(everyone, psend.at[peer], precv.at[samp], sem_p, peer))

    loop(NZ, layer_step)
    precv[samp] = psend[samp]

    loop(SP // W, lambda i: stack(res_ref[:, block(i, W)], i))
    TW = min(TV, 256)

    def ascore(i):
        cols = block(i, TW)
        apart[:, cols] = sum3(jnp.dot(parts[...], tbf[:, cols], preferred_element_type=F32))

    loop(TV // TW, ascore)
    spots = []
    for i in range(NJ):
        h, q = divmod(i, quarters)
        spots.append((slice(8 * h, 8 * h + 8), slice(128 * q, 128 * q + 128)))
    for i, spot in enumerate(spots):
        asend[i] = apart[spot]
    each_peer(near, lambda peer: push(near, asend.at[peer], arecv.at[j], sem_a, peer))
    arecv[j] = asend[j]

    arrived(everyone, precv.at[pl.ds(0, NS - 1)], sem_p)
    total = precv[0]
    for i in range(1, NS):
        total = total + precv[i]
    pall[samp] = total

    def share_sums(t):
        each_in_plane(t, lambda peer: push(everyone, pall.at[samp], pall.at[samp], sem_pa, peer, 2 - t // (NZ - 1)))

    loop(NZ, share_sums)

    arrived(near, arecv.at[pl.ds(0, NJ - 1)], sem_a)
    total = arecv[0]
    for i in range(1, NJ):
        total = total + arecv[i]
    az[z] = total
    each_peer(over_z, lambda peer: push(over_z, az.at[z], az.at[z], sem_az, peer))
    def scaled(layer, place):
        for k in range(NY):
            chip = layer * NY + k
            sums = jnp.concatenate([pall[2 * chip], pall[2 * chip + 1]], axis=0) * squares[chip]
            for i, part in enumerate(split3(sums)):
                lefts[place, 16 * i : 16 * i + 16, k * 128 : (k + 1) * 128] = part

    def against(place, rows):
        return lax.dot_general(
            lefts[place], gbf[rows, block((z + place) % NZ, VZ)], (((1,), (1,)), ((), ())), preferred_element_type=F32
        )

    arrived(everyone, pall.at[pl.ds(0, NJ - 1)], sem_pa, 1)
    scaled(z, 0)

    def own_parts(i):
        for q in (2 * i, 2 * i + 1):
            acc[q] = against(0, block(q, SQ))

    loop(NX // 2, own_parts)
    arrived(everyone, pall.at[pl.ds(0, NS - NJ)], sem_pa, 2)
    loop(NZ - 1, lambda k: scaled((z + k + 1) % NZ, k + 1))

    def part(q):
        total = acc[q]
        for k in range(1, NZ):
            total = total + against(k, block(q, SQ))
        value = sum3(total)
        for c in range(CW):
            cols = slice(c * W, (c + 1) * W)
            isend[q, :, cols] = (
                vc_ref[1] * value[0:8, cols] + vc_ref[2] * shuf[q * CW + c] * value[8:16, cols]
            ) * (1.0 / scale_rows)
        each_peer(over_x, lambda peer: push(over_x, isend.at[q], irecv.at[q, x], sem_im.at[q], peer))
        irecv[q, x] = isend[q]

    loop(NX, part)

    arrived(over_z, az.at[pl.ds(0, NZ - 1)], sem_az)
    total = az[0]
    for i in range(1, NZ):
        total = total + az[i]
    aall[j] = total
    each_peer(near, lambda peer: push(near, aall.at[j], aall.at[j], sem_aa, peer))
    sent(over_z, table.at[pl.ds(0, NZ - 1)], sem_ez)
    sent(near, table.at[pl.ds(0, 28)], sem_ej)
    sent(over_x, shuf.at[pl.ds(0, CW * (NX - 1))], sem_sh)
    sent(everyone, psend.at[pl.ds(0, NS - 1)], sem_p)
    sent(everyone, pall.at[pl.ds(0, NS - 1)], sem_pa)
    sent(near, asend.at[pl.ds(0, NJ - 1)], sem_a)
    bpart[...] = jnp.zeros_like(bpart)

    def score(q, sums):
        arrived(over_x, irecv.at[q, pl.ds(0, NX - 1)], sem_im.at[q])
        image = irecv[q, 0]
        for i in range(1, NX):
            image = image + irecv[q, i]
        cols = block(q, SQ)
        d, r = dir_ref[:, cols], res_ref[:, cols]
        image = vc_ref[0] * d + image
        image_ref[:, cols] = image
        for c in range(CW):
            stack(image[:, c * W : (c + 1) * W], q * CW + c)
        bpart[...] += sum3(jnp.dot(parts[:, cols], tbf[cols, :], preferred_element_type=F32))
        sums = list(sums)
        for k, term in enumerate((r * r, d * image, r * image, image * image)):
            for c in range(SQ // 128):
                sums[k] = sums[k] + term[:, 128 * c : 128 * c + 128]
        return tuple(sums)

    sums = lax.fori_loop(0, NX, score, (jnp.zeros((8, 128), F32),) * 4)
    lane = lax.broadcasted_iota(jnp.int32, (8, 128), 1) - lax.broadcasted_iota(jnp.int32, (8, 128), 0)
    scalars = jnp.zeros((8, 128), F32)
    for k in range(4):
        scalars = jnp.where(lane == 8 * k, jnp.sum(sums[k], axis=1, keepdims=True), scalars)
    scalars = jnp.broadcast_to(jnp.sum(scalars, axis=0, keepdims=True), (8, 128))
    for i, spot in enumerate(spots):
        fsend[i, 0] = bpart[spot]
        fsend[i, 1] = scalars
    each_peer(near, lambda peer: push(near, fsend.at[peer], frecv.at[j], sem_f, peer))
    frecv[j] = fsend[j]
    for q in range(NX):
        sent(over_x, isend.at[pl.ds(0, NX - 1)], sem_im.at[q])
    arrived(near, frecv.at[pl.ds(0, NJ - 1)], sem_f)
    total = frecv[0]
    for i in range(1, NJ):
        total = total + frecv[i]
    fall[samp] = total[0]
    sums_z[z] = total[1]
    each_peer(everyone, lambda peer: push(everyone, fall.at[samp], fall.at[samp], sem_fa, peer))
    each_peer(over_z, lambda peer: push(over_z, sums_z.at[z], sums_z.at[z], sem_sz, peer))
    arrived(over_z, sums_z.at[pl.ds(0, NZ - 1)], sem_sz)
    row = sums_z[0]
    for i in range(1, NZ):
        row = row + sums_z[i]
    norm_now, curvature, cross, square = (
        jnp.sum(jnp.where(lane == 8 * k, row, 0.0), axis=1, keepdims=True) for k in range(4)
    )
    alpha = norm_now / curvature

    norm_next = norm_now - 2.0 * alpha * cross + alpha * alpha * square
    beta = norm_next / norm_now
    d = dir_ref[...]
    new_res = res_ref[...] - alpha * image_ref[...]
    osol_ref[...] = sol_ref[...] + alpha * d
    ores_ref[...] = new_res
    odir_ref[...] = new_res + beta * d
    sent(near, fsend.at[pl.ds(0, NJ - 1)], sem_f)
    sent(over_z, sums_z.at[pl.ds(0, NZ - 1)], sem_sz)

    tfreq = tpct / 100.0
    root = float(NS * SP) ** 0.5 * 50.0
    tscale = lax.rsqrt(2.0 * tfreq * (1.0 - tfreq)) / root
    arrived(everyone, fall.at[pl.ds(0, NS - 1)], sem_fa)
    sent(over_z, az.at[pl.ds(0, NZ - 1)], sem_az)
    sent(near, aall.at[pl.ds(0, NJ - 1)], sem_aa)
    arrived(near, aall.at[pl.ds(0, NJ - 1)], sem_aa)
    for i, spot in enumerate(spots):
        total = fall[i]
        for k in range(1, NZ):
            total = total + fall[k * NJ + i]
        oassoc_ref[spot] = (aall[i] - alpha * total) * tscale[:, spot[1]]
    sent(everyone, fall.at[pl.ds(0, NS - 1)], sem_fa)


def local(dims, geno, allele_pct, test_geno, test_pct, exposure, perm, var_comp, solution, resid, direction):
    NZ, NJ, NX, _ = dims
    SP, V = geno.shape
    TV = test_geno.shape[1]
    RP, VB, SQ = SP // 128, V // NJ, SP // NX
    W = min(SQ, 256)
    chunks, tchunks = 4, 1
    NS = NZ * NJ
    vmem = pl.BlockSpec(memory_space=pltpu.VMEM)
    hbm = pl.BlockSpec(memory_space=pltpu.HBM)
    dma = pltpu.SemaphoreType.DMA
    rhs = jax.ShapeDtypeStruct((8, SP), F32)
    outs = (rhs, rhs, rhs, jax.ShapeDtypeStruct((16, TV), F32))
    results = pl.pallas_call(
        functools.partial(kernel, dims),
        out_shape=outs,
        in_specs=[hbm] * 10,
        out_specs=(vmem, vmem, vmem, vmem),
        scratch_shapes=[
            pltpu.SMEM((3,), F32),
            pltpu.VMEM((8, SP), jnp.int32),
            pltpu.VMEM((1, V), jnp.int32),
            pltpu.VMEM((1, TV), jnp.int32),
            pltpu.VMEM((8, SP), F32),
            pltpu.VMEM((8, SP), F32),
            pltpu.VMEM((8, SP), F32),
            pltpu.VMEM((chunks, SP // chunks, V), jnp.int32),
            pltpu.VMEM((tchunks, SP // tchunks, TV), jnp.int32),
            pltpu.VMEM((SP, V), BF16),
            pltpu.VMEM((SP, TV), BF16),
            pltpu.VMEM((NS, RP, 128), F32),
            pltpu.VMEM((384, NS * RP // 2), BF16),
            pltpu.VMEM((8, 1, SQ), jnp.int32),
            pltpu.VMEM((8, 1, SQ), jnp.int32),
            pltpu.VMEM((SP // W, 8, W), F32),
            pltpu.VMEM((48, SP), BF16),
            pltpu.VMEM((NZ, 48, V // NZ), BF16),
            pltpu.VMEM((V // 128, 1, 128), F32),
            pltpu.VMEM((NJ, 48, VB), F32),
            pltpu.VMEM((NX, 48, SQ), F32),
            pltpu.VMEM((8, SP), F32),
            pltpu.VMEM((16, TV), F32),
            pltpu.VMEM((16, TV), F32),
            pltpu.VMEM((NS, 8, 128), F32),
            pltpu.VMEM((NS, 8, 128), F32),
            pltpu.VMEM((NS, 8, 128), F32),
            pltpu.VMEM((NJ, 8, 128), F32),
            pltpu.VMEM((NJ, 8, 128), F32),
            pltpu.VMEM((NZ, 8, 128), F32),
            pltpu.VMEM((NJ, 8, 128), F32),
            pltpu.VMEM((NX, NX, 8, SQ), F32),
            pltpu.VMEM((NX, 8, SQ), F32),
            pltpu.VMEM((NJ, 2, 8, 128), F32),
            pltpu.VMEM((NJ, 2, 8, 128), F32),
            pltpu.VMEM((NS, 8, 128), F32),
            pltpu.VMEM((NZ, 8, 128), F32),
            dma((8,)),
            dma((chunks,)),
            dma((tchunks,)),
            dma((2,)),
            dma((4,)),
            dma((2,)),
            dma((2,)),
            dma((3,)),
            dma((2,)),
            dma((2,)),
            dma((2,)),
            dma((NX, 2)),
            dma((2,)),
            dma((2,)),
            dma((2,)),
        ],
        compiler_params=pltpu.CompilerParams(
            collective_id=0, has_side_effects=True, vmem_limit_bytes=40 * 1024 * 1024
        ),
    )(
        *(
            pltpu.with_memory_space_constraint(value, pltpu.HBM)
            for value in (
                geno,
                test_geno,
                allele_pct.reshape(1, V),
                test_pct.reshape(1, TV),
                exposure.reshape(RP, 128),
                perm,
                var_comp,
                solution,
                resid,
                direction,
            )
        )
    )
    return pl.pallas_call(
        hand_over,
        out_shape=outs,
        in_specs=[vmem] * 4,
        out_specs=(vmem,) * 4,
        compiler_params=pltpu.CompilerParams(vmem_limit_bytes=2 * 1024 * 1024),
    )(*results)


def hand_over(*refs):
    for source, target in zip(refs[:4], refs[4:]):
        target[...] = source[...]


def solution(mesh):
    samp, var = mesh.shape["samp"], mesh.shape["var"]
    near = 8 if samp == 32 else samp // 2

    def whole(geno, *rest):
        dims = (samp // near, near, var, float(geno.shape[1]))
        return jax.shard_map(
            functools.partial(local, dims),
            mesh=mesh,
            in_specs=(
                P("samp", "var"),
                P("var"),
                P("samp", "var"),
                P("var"),
                P("samp"),
                P(None, "samp"),
                P(),
                P(None, "samp"),
                P(None, "samp"),
                P(None, "samp"),
            ),
            out_specs=(P(None, "samp"), P(None, "samp"), P(None, "samp"), P(None, "var")),
            check_vma=False,
        )(geno, *rest)

    return whole
```
